256 devices in a mesh: section: 8 (over x, core), expert: 32 (over y, z).
Axes of the slice: x: 4, y: 4, z: 8, core: 2. Of those that a mesh axis runs over, the one named last changes fastest.
Arguments:
- hidden_in: bfloat16 [8, 128, 4096], P('section', 'expert'), may hold values from -4 to 4
- attn_gain: bfloat16 [8, 4096], P('section'), may hold values from 0.5 to 2
- w_query: bfloat16 [8, 4096, 4096], P('section', None, 'expert'), may hold values from -0.09375 to 0.09375
- w_out: bfloat16 [8, 4096, 4096], P('section', None, 'expert'), may hold values from -0.09375 to 0.09375
- key_cache: bfloat16 [8, 3, 128, 64, 4, 128], P('section', None, 'expert'), may hold values from -2 to 2
- value_cache: bfloat16 [8, 3, 128, 64, 4, 128], P('section', None, 'expert'), may hold values from -6 to 6
- lengths: int32 [8, 3, 128], P('section', None, 'expert'), may hold values from 1 to 64, 4096 in all within a row
- ffn_gain: bfloat16 [8, 4096], P('section'), may hold values from 0.5 to 2
- w_gate: bfloat16 [8, 32, 4096, 384], P('section', 'expert'), may hold values from -0.09375 to 0.09375
- w_up: bfloat16 [8, 32, 4096, 384], P('section', 'expert'), may hold values from -0.09375 to 0.09375
- w_down: bfloat16 [8, 32, 384, 4096], P('section', 'expert'), may hold values from -0.21875 to 0.21875
- routes: int32 [8, 3, 128, 8], P('section', None, 'expert'), may hold values from 0 to 15, all different within a row; in each aligned block of 4 rows (0 to 3, 4 to 7, ..., all dimensions but the last counted through in order) at most 4 rows name the same one
- gates: float32 [8, 3, 128, 8], P('section', None, 'expert'), may hold values from 0.1 to 1
Outputs:
- out: bfloat16 [8, 128, 4096], P('section', 'expert')
The draws below stay inside these ranges and needn't reach their ends.
Inputs may be any that keep to these rules, and one draw needn't show every extreme that they name: `routes`: each row names 8 different experts of the 16; among the 4 rows that one index of the expert axis holds at one section and step, an expert is named by at most 4 rows.
All inputs are finite; a program needn't handle non-finite values. No bound on the sum of `lengths` on one device may be relied on, other than what follows from the above.
Results may differ from the reference program's by a relative error of at most 0.04.
Values may be sent and summed in bfloat16 or wider, within the bound.
A program may use at most 64 MiB of HBM per device.

```python
import math
import jax
import jax.numpy as jnp
import numpy as np
from jax import lax

D = 4096
HD = 128
HQ = 32
KVH = 4
FFE = 768
FFD = 384
ROWS_DEV = 4
CACHE = 64
STEPS = 3
SECTIONS = 8
EXPERTS = 16
TOPK = 8
ROWS = 128


def draw_hidden_in(key, part):
    base_key, row_key, col_key = jax.random.split(key, 3)
    full_shape = (SECTIONS, ROWS, D)
    base_values = jnp.clip(jax.random.normal(base_key, full_shape, jnp.float32), -4.0, 4.0)
    log_low = math.log(0.1)
    row_scale = jnp.exp(jax.random.uniform(row_key, (SECTIONS, ROWS, 1), jnp.float32, log_low, 0.0))
    col_scale = jnp.exp(jax.random.uniform(col_key, (1, 1, D), jnp.float32, log_low, 0.0))
    return (base_values * row_scale * col_scale).astype(jnp.bfloat16)


def levels(key, shape, pieces, low, high):
    factor_of = 1.0
    for dim, blocks in pieces:
        steps = jax.random.uniform(jax.random.fold_in(jax.random.fold_in(key, 6), dim), (blocks,), jnp.float32, low / len(pieces), high / len(pieces))
        factor_of = factor_of * jnp.repeat(jnp.exp(steps), shape[dim] // blocks).reshape((-1,) + (1,) * (len(shape) - 1 - dim))
    return factor_of


def profile(number_of, total, bound, skew):
    portions = [(1 << 20) // math.isqrt(standing ** skew) + 1 for standing in range(2, number_of + 1)]
    rest, holding = total - bound - (number_of - 1), [1] * (number_of - 1)
    while rest > 0:
        free = [i for i in range(number_of - 1) if holding[i] < bound]
        pool, left = sum([portions[i] for i in free]), rest
        for i in free:
            extra = min(bound - holding[i], max(1, left * portions[i] // pool), rest)
            holding[i] = holding[i] + extra
            rest = rest - extra
    return np.array([bound] + holding)


def ragged(stream_key, amount, total, bound, lean):
    if amount == 2:
        one = jax.random.randint(stream_key, (), max(1, total - bound), min(bound, total - 1) + 1)
        return jnp.stack([one, total - one])
    tallies = jnp.asarray(profile(amount, total, bound, lean), jnp.int32)
    twos = (amount - 1) // 2
    giver, taker = tallies[1:1 + 2 * twos:2], tallies[2:2 + 2 * twos:2]
    slack = jnp.minimum(giver - 1, bound - taker)
    passed = jax.random.randint(jax.random.fold_in(stream_key, 1), (twos,), 0, 1 << 20) % (slack + 1)
    tallies = tallies.at[1:1 + 2 * twos:2].set(giver - passed).at[2:2 + 2 * twos:2].set(taker + passed)
    return tallies[jax.random.permutation(jax.random.fold_in(stream_key, 2), amount)]


def routed_block(rng, own, number, rows, number_of, top, bound, slope):
    sequence = jax.random.permutation(rng, number_of)
    heavy_load, usual = portions_of(number_of, rows * top, bound, slope, True), portions_of(number_of, rows * top, bound, slope, False)
    places = jnp.arange(number_of)

    def named(sizes, offset_by):
        used = int((sizes > 0).sum())
        fixed = max(1, used // 4)
        passed = fixed + (places - fixed + offset_by * (used - fixed)) % max(1, number_of - fixed)
        return jnp.zeros((number_of,), jnp.int32).at[sequence[jnp.where(places < fixed, places, passed)]].set(jnp.asarray(sizes, jnp.int32))

    sizes = jnp.where(number % 4 == 0, named(heavy_load, number // 4), named(usual, number - number // 4 - 1))
    mixed = jax.random.permutation(jax.random.fold_in(own, 3), number_of)
    giver, taker = mixed[0:number_of // 2 * 2:2], mixed[1:number_of // 2 * 2:2]
    slack = jnp.minimum(sizes[giver] - 1, bound - sizes[taker]) // 2
    slack = jnp.where((giver == sequence[0]) | (taker == sequence[0]) | (sizes[taker] == 0), 0, jnp.maximum(slack, 0))
    passed = jax.random.randint(jax.random.fold_in(own, 4), (number_of // 2,), 0, 1 << 20) % (slack + 1)
    sizes = sizes.at[giver].add(-passed).at[taker].add(passed)
    labels = jnp.searchsorted(jnp.cumsum(sizes), jnp.arange(rows * top), side="right").astype(jnp.int32)
    grid = labels.reshape(top, rows).T
    grid = grid[jax.random.permutation(jax.random.fold_in(own, 1), rows)]
    offset_by = jax.random.randint(jax.random.fold_in(own, 2), (rows, 1), 0, top)
    return jnp.take_along_axis(grid, (jnp.arange(top)[None, :] + offset_by) % top, axis=1)


def portions_of(number_of, total, reach, lean, full):
    loads = [(1 << 20) // math.isqrt(grade ** lean) + 1 for grade in range(1, number_of + 1)]
    largest = reach if full else min(reach, max(-(-total // number_of), total * loads[0] // sum(loads)))
    least = 1 if total - largest >= number_of - 1 else 0
    counts, rest = [largest] + [least] * (number_of - 1), total - largest - least * (number_of - 1)
    while rest > 0:
        free = [i for i in range(1, number_of) if counts[i] < largest] or [i for i in range(1, number_of) if counts[i] < reach]
        mass, left = sum([loads[i] for i in free]), rest
        for i in free:
            addition = min(reach - counts[i], max(1, left * loads[i] // mass), rest)
            counts[i] = counts[i] + addition
            rest = rest - addition
    return np.array(counts)


def scatter_about(stream_key, dims, width, bound, cuts=(), kind=jnp.bfloat16):
    entries = jax.random.normal(stream_key, dims, jnp.float32) * width
    if len(cuts) > 0:
        entries = levels(stream_key, dims, cuts, -0.22, 0.18) * entries
    return jnp.clip(entries, min=-bound, max=bound).astype(kind)


def setup_inputs(seed: int = 0) -> dict:
    arg_keys = jax.random.split(jax.random.key(seed), 14)
    hidden_in = draw_hidden_in(jax.random.fold_in(arg_keys[13], 71), 0)
    attn_gain = jnp.clip(jnp.exp(math.log(2.0) - 1.3862944 * jax.random.uniform(arg_keys[1], (SECTIONS, D), jnp.float32) ** levels(arg_keys[1], (SECTIONS, D), ((0, 8),), -0.2, 0.2)), 0.5, 2.0).astype(jnp.bfloat16)
    w_query = scatter_about(arg_keys[2], (SECTIONS, D, HQ * HD), D ** -0.5, 0.09375, ((0, 8), (2, 32)))
    w_out = scatter_about(arg_keys[3], (SECTIONS, HQ * HD, D), (HQ * HD) ** -0.5, 0.09375, ((0, 8), (2, 32)))
    key_cache = jnp.clip(jax.random.uniform(arg_keys[4], (SECTIONS, STEPS, ROWS, CACHE, KVH, HD), jnp.float32, -2.0, 2.0) * levels(arg_keys[4], (SECTIONS, STEPS, ROWS, CACHE, KVH, HD), ((0, 8), (2, 32)), -0.4, 0.0), -2.0, 2.0).astype(jnp.bfloat16)
    value_cache = scatter_about(arg_keys[5], (SECTIONS, STEPS, ROWS, CACHE, KVH, HD), 1.0, 6.0, ((0, 8), (2, 32)))
    lengths = jax.vmap(lambda own: ragged(own, ROWS, ROWS * CACHE // 2, CACHE, 2))(jax.random.split(arg_keys[6], SECTIONS * STEPS)).reshape((SECTIONS, STEPS, ROWS)).astype(jnp.int32)
    ffn_gain = jnp.clip(jnp.exp(math.log(2.0) - 1.3862944 * jax.random.uniform(arg_keys[7], (SECTIONS, D), jnp.float32) ** levels(arg_keys[7], (SECTIONS, D), ((0, 8),), -0.2, 0.2)), 0.5, 2.0).astype(jnp.bfloat16)
    w_gate = scatter_about(arg_keys[8], (SECTIONS, 2 * EXPERTS, D, FFD), D ** -0.5, 0.09375, ((0, 8), (1, 32)))
    w_up = scatter_about(arg_keys[9], (SECTIONS, 2 * EXPERTS, D, FFD), D ** -0.5, 0.09375, ((0, 8), (1, 32)))
    w_down = scatter_about(arg_keys[10], (SECTIONS, 2 * EXPERTS, FFD, D), FFE ** -0.5, 0.21875, ((0, 8), (1, 32)))
    routes_keys = jax.random.split(jax.random.fold_in(arg_keys[11], 1), SECTIONS * STEPS * ROWS // ROWS_DEV)
    routes_turns = jax.random.permutation(jax.random.fold_in(arg_keys[11], 3), SECTIONS * STEPS * ROWS // ROWS_DEV)
    routes = jax.vmap(lambda own, number: routed_block(jax.random.fold_in(arg_keys[11], 2), own, number, ROWS_DEV, EXPERTS, TOPK, ROWS_DEV, 2))(routes_keys, routes_turns).reshape((SECTIONS, STEPS, ROWS, TOPK))
    gates = jnp.clip(jnp.exp(math.log(1.0) - 2.3025851 * jax.random.uniform(arg_keys[12], (SECTIONS, STEPS, ROWS, TOPK), jnp.float32) ** levels(arg_keys[12], (SECTIONS, STEPS, ROWS, TOPK), ((0, 8), (2, 32)), -0.2, 0.2)), 0.1, 1.0)
    return {"hidden_in": hidden_in, "attn_gain": attn_gain, "w_query": w_query, "w_out": w_out, "key_cache": key_cache, "value_cache": value_cache, "lengths": lengths, "ffn_gain": ffn_gain, "w_gate": w_gate, "w_up": w_up, "w_down": w_down, "routes": routes, "gates": gates}


def rms_scaled(values):
    return values * lax.rsqrt(lax.optimization_barrier(jnp.mean(values * values, axis=-1, keepdims=True)) + 1e-06)

def one_layer(hidden_state, gain_attn, query_w, out_w, cache_keys, cache_values, row_lengths, gain_ffn, gate_w, up_w, down_w, route_ids, gate_vals):
    state32 = hidden_state.astype(jnp.float32)
    normed = (rms_scaled(state32) * gain_attn.astype(jnp.float32)).astype(jnp.bfloat16)
    queries = jnp.dot(normed, query_w, preferred_element_type=jnp.float32).reshape(ROWS, HQ, HD)
    q_normed = rms_scaled(queries).astype(jnp.bfloat16).reshape(ROWS, KVH, HQ // KVH, HD)
    scores = jnp.einsum('mkgd,mpkd->mkgp', q_normed.astype(jnp.float32), cache_keys.astype(jnp.float32)) * HD ** (-0.5)
    in_cache = jnp.arange(CACHE, dtype=jnp.int32)[None, :] < row_lengths[:, None]
    exp_scores = jnp.where(in_cache[:, None, None, :], jnp.exp(scores), 0.0)
    weights = (exp_scores / lax.optimization_barrier(jnp.sum(exp_scores, axis=-1, keepdims=True))).astype(jnp.bfloat16)
    context = jnp.einsum('mkgp,mpkd->mkgd', weights.astype(jnp.float32), cache_values.astype(jnp.float32))
    context = context.astype(jnp.bfloat16).reshape(ROWS, HQ * HD)
    middle = state32 + jnp.dot(context, out_w, preferred_element_type=jnp.float32)
    ffn_in = (rms_scaled(middle) * gain_ffn.astype(jnp.float32)).astype(jnp.bfloat16)
    shares = gate_vals / lax.optimization_barrier(jnp.sum(gate_vals, axis=-1, keepdims=True))
    chosen = route_ids[:, :, None] == jnp.arange(EXPERTS, dtype=jnp.int32)[None, None, :]
    coeffs = lax.optimization_barrier(jnp.sum(jnp.where(chosen, shares[:, :, None], 0.0), axis=1))

    def half_expert(weights_half):
        gate_half, up_half, down_half = weights_half
        gate_val = jnp.dot(ffn_in, gate_half, preferred_element_type=jnp.float32)
        up_val = jnp.dot(ffn_in, up_half, preferred_element_type=jnp.float32)
        active = (jax.nn.silu(gate_val) * up_val).astype(jnp.bfloat16)
        return jnp.dot(active, down_half, preferred_element_type=jnp.float32).astype(jnp.bfloat16)
    halves = lax.map(half_expert, (gate_w, up_w, down_w))
    paired = lax.optimization_barrier(jnp.sum(halves.astype(jnp.float32).reshape(EXPERTS, 2, ROWS, D), axis=1)).astype(jnp.bfloat16)
    paired = lax.optimization_barrier(paired).astype(jnp.float32)
    expert_sum = jnp.einsum('me,emd->md', coeffs, paired, precision=lax.Precision.HIGHEST)
    return (middle + expert_sum).astype(jnp.bfloat16)

def reference(hidden_in, attn_gain, w_query, w_out, key_cache, value_cache, lengths, ffn_gain, w_gate, w_up, w_down, routes, gates):
    states = hidden_in

    def apply_section(packed):
        return one_layer(packed[12], packed[0], packed[1], packed[2], packed[7], packed[8], packed[9], packed[3], packed[4], packed[5], packed[6], packed[10], packed[11])
    for layer_step in range(STEPS):
        results = lax.map(apply_section, (attn_gain, w_query, w_out, ffn_gain, w_gate, w_up, w_down, key_cache[:, layer_step], value_cache[:, layer_step], lengths[:, layer_step], routes[:, layer_step], gates[:, layer_step], states))
        if layer_step + 1 < STEPS:
            states = jnp.roll(results, 1, axis=0)
        else:
            states = results
    return states
```

```python
import jax
import jax.numpy as jnp
from jax import lax
from jax.experimental import pallas as pl
from jax.experimental.pallas import tpu as pltpu
from jax.sharding import PartitionSpec as P

STEPS = 3
NY = 4
NZ = 8
EPS = 1e-06
NEAR_FIRST = (0, 1, 7, 2, 6, 3, 5, 4)
FAR_FIRST = (4, 3, 5, 2, 6, 1, 7, 0)
BF = jnp.bfloat16
F32 = jnp.float32
MESH = pl.DeviceIdType.MESH


def remote(src, dst, send, recv, peer):
    return pltpu.make_async_remote_copy(
        src_ref=src, dst_ref=dst, send_sem=send, recv_sem=recv, device_id=peer, device_id_type=MESH
    )


def pieces_to_rows(pieces, rows):
    for i in range(pieces.shape[0]):
        rows[4 * i : 4 * i + 4, :] = pieces[i].astype(F32)


def kernel(
    hid, meta, again, fgain, wq, wo, wg, wu, wd, kt, vt,
    out,
    wq_v, wo_v, wgu_v, wd_v, ga_v, gf_v, kbuf, vbuf,
    hbuf, mbuf, rows, mrows, grid, qsend, qbuf, part, half_in, full_out, full_in, ysum, zin,
    mid, acc, act, osend, obuf,
    load_sem, kv_own, kv_send, kv_recv, sm_own, sm_send, sm_recv,
    z_send, z_recv, y_send, y_recv, h_send, h_recv,
    q_own, q_snd, q_rcv, rh_send, rh_recv, rf_send, rf_recv, rz_send, rz_recv,
    hop_send, hop_recv, o_sem,
):
    e = lax.axis_index("expert")
    s = lax.axis_index("section")
    y, z = e // NZ, e % NZ
    nsec = lax.axis_size("section")
    n = NY * NZ
    nxt, prv = (s + 1) % nsec, (s + nsec - 1) % nsec
    up, down, far = (y + 1) % NY, (y + NY - 1) % NY, (y + 2) % NY

    def dev(yy, zz):
        return {"expert": yy * NZ + zz}

    loads = [
        pltpu.make_async_copy(wq, wq_v, load_sem.at[0]),
        pltpu.make_async_copy(again, ga_v, load_sem.at[1]),
        pltpu.make_async_copy(wo, wo_v, load_sem.at[2]),
        pltpu.make_async_copy(fgain, gf_v, load_sem.at[3]),
        pltpu.make_async_copy(wg, wgu_v.at[:, 0:384], load_sem.at[4]),
        pltpu.make_async_copy(wu, wgu_v.at[:, 384:768], load_sem.at[5]),
        pltpu.make_async_copy(wd, wd_v, load_sem.at[6]),
    ]
    for c in loads:
        c.start()

    barrier = pltpu.get_barrier_semaphore()

    def greet(d, _):
        pl.semaphore_signal(barrier, inc=1, device_id={"expert": (e + d) % n}, device_id_type=MESH)
        return 0

    lax.fori_loop(1, n, greet, 0)
    pl.semaphore_signal(barrier, inc=1, device_id={"section": nxt}, device_id_type=MESH)
    pl.semaphore_signal(barrier, inc=1, device_id={"section": prv}, device_id_type=MESH)
    pl.semaphore_wait(barrier, n + 1)

    def hid_copy(p):
        return remote(
            hid.at[:, pl.ds(pl.multiple_of(128 * p, 128), 128)], hbuf.at[z * NY + y],
            sm_send.at[0], sm_recv.at[0], {"expert": p},
        )

    def meta_copy(p):
        return remote(meta, mbuf.at[z * NY + y], sm_send.at[1], sm_recv.at[1], {"expert": p})

    def send_start(d, _):
        p = (e + d) % n
        hid_copy(p).start()
        return 0

    def send_meta(d, _):
        meta_copy((e + d) % n).start()
        return 0

    own_h = pltpu.make_async_copy(
        hid.at[:, pl.ds(pl.multiple_of(128 * e, 128), 128)], hbuf.at[z * NY + y], sm_own.at[0]
    )
    own_m = pltpu.make_async_copy(meta, mbuf.at[z * NY + y], sm_own.at[1])
    own_h.start()
    own_m.start()
    lax.fori_loop(1, n, send_start, 0)
    lax.fori_loop(1, n, send_meta, 0)

    def kv_copies(t, d):
        yy = (y + d) % NY
        return (
            remote(kt.at[yy, t], kbuf.at[t, y], kv_send.at[0, t, d], kv_recv.at[0, t, d], dev(yy, z)),
            remote(vt.at[yy, t], vbuf.at[t, y], kv_send.at[1, t, d], kv_recv.at[1, t, d], dev(yy, z)),
        )

    def kv_owns(t):
        return (
            pltpu.make_async_copy(kt.at[y, t], kbuf.at[t, y], kv_own.at[0, t]),
            pltpu.make_async_copy(vt.at[y, t], vbuf.at[t, y], kv_own.at[1, t]),
        )

    for t in range(STEPS):
        for c in kv_owns(t):
            c.start()
    for t in range(STEPS):
        for d in range(1, NY):
            for c in kv_copies(t, d):
                c.start()

    def many(ref, k, send, recv):
        view = ref.at[pl.ds(0, k)]
        return remote(view, view, send, recv, {"expert": (e + 1) % n})

    own_h.wait()
    many(hbuf, n - 1, sm_send.at[0], sm_recv.at[0]).wait_recv()
    pieces_to_rows(hbuf, rows)
    grid[0, 0, z, y] = rows[...].astype(BF)
    own_m.wait()
    many(mbuf, n - 1, sm_send.at[1], sm_recv.at[1]).wait_recv()
    pieces_to_rows(mbuf, mrows)

    def gather(g, t, consume):
        def z_copy(d):
            b = grid.at[g, t, z, y]
            return remote(b, b, z_send.at[g, d], z_recv.at[g, t, d], dev(y, (z + d) % NZ))

        def src(d):
            return (z + NZ - d) % NZ

        def y_copy(d, way):
            b = grid.at[g, t, src(d), y]
            to = up if way == 0 else down
            return remote(b, b, y_send.at[g, d, way], y_recv.at[g, t, d, way], dev(to, z))

        def h_copy(d, way):
            frm, to = (down, up) if way == 0 else (up, down)
            b = grid.at[g, t, src(d), frm, pl.ds(64 * way, 64)]
            return remote(b, b, h_send.at[g, d, way], h_recv.at[g, t, d, way], dev(to, z))

        for d in NEAR_FIRST[1:]:
            z_copy(d).start()
        for k in range(NZ + 2):
            if k < NZ:
                d = NEAR_FIRST[k]
                if d:
                    z_copy(d).wait_recv()
                y_copy(d, 0).start()
                y_copy(d, 1).start()
            if 1 <= k <= NZ:
                d = NEAR_FIRST[k - 1]
                for way in range(2):
                    y_copy(d, way).wait_recv()
                    h_copy(d, way).start()
            if k >= 2:
                d = NEAR_FIRST[k - 2]
                for way in range(2):
                    h_copy(d, way).wait_recv()
                consume(src(d))

        def drain():
            for d in NEAR_FIRST:
                if d:
                    z_copy(d).wait_send()
                for way in range(2):
                    y_copy(d, way).wait_send()
                    h_copy(d, way).wait_send()

        return drain

    def column_start(zs, yy):
        return pl.multiple_of(128 * (yy * NZ + zs), 128)

    def scaled_block(g, t, gain_v, zs):
        xs = [grid[g, t, zs, yy].astype(F32) for yy in range(NY)]
        total = sum(jnp.sum(x * x, axis=1, keepdims=True) for x in xs)
        parts = [
            (xs[yy] * gain_v[:, pl.ds(column_start(zs, yy), 128)].astype(F32)).astype(BF) for yy in range(NY)
        ]
        return total, jnp.concatenate(parts, axis=1)

    def weight_rows(w, zs):
        return jnp.concatenate([w[pl.ds(column_start(zs, yy), 128), :] for yy in range(NY)], axis=0)

    lane = lax.broadcasted_iota(jnp.int32, (128, 128), 1)

    def meta_column(index):
        return jnp.sum(jnp.where(lane == index, mrows[...], 0.0), axis=1, keepdims=True)

    d_model = NY * NZ * 128

    def step(t, carry):
        @pl.when(t > 0)
        def _():
            b = grid.at[0, t, z, y]
            remote(b, b, hop_send.at[t], hop_recv.at[t], {"section": nxt}).wait_recv()

        @pl.when(t == 0)
        def _():
            for c in loads[0:2]:
                c.wait()

        sums = jnp.zeros((128, 1), F32)
        acc[:, 0:128] = jnp.zeros((128, 128), F32)
        acc[:, 128:256] = jnp.zeros((128, 128), F32)

        def take_query(zs):
            total, lhs = scaled_block(0, t, ga_v, zs)
            acc[:, 0:128] += jnp.dot(lhs, weight_rows(wq_v, zs), preferred_element_type=F32)
            acc[:, 128:256] += jnp.broadcast_to(total, (128, 128))

        drain_a = gather(0, t, take_query)
        scale = lax.rsqrt(acc[:, 128:256] / d_model + EPS)
        query = acc[:, 0:128] * scale
        query = query * lax.rsqrt(jnp.mean(query * query, axis=1, keepdims=True) + EPS)
        qsend[t] = query.astype(BF).reshape(NZ, 16, 128)

        def q_copy(d):
            zz = (z + d) % NZ
            return remote(qsend.at[t, zz], qbuf.at[t, z], q_snd, q_rcv.at[t], dev(y, zz))

        own_q = pltpu.make_async_copy(qsend.at[t, z], qbuf.at[t, z], q_own)
        own_q.start()
        for d in (4, 3, 5, 2, 6, 1, 7):
            q_copy(d).start()

        for c in kv_owns(t):
            c.wait()
        for d in range(1, NY):
            for c in kv_copies(t, d):
                c.wait_recv()
        length = meta_column(64 + t)
        pos = lax.broadcasted_iota(jnp.int32, (128, 128), 0)
        pick = jnp.where(lane == z * 16 + pos % 16, 1.0, 0.0)
        own_len = jnp.dot(pick, length * jnp.ones((1, 128), F32), precision=lax.Precision.HIGHEST)[:, 0:1]
        key_lane = lax.broadcasted_iota(jnp.int32, (128, 1024), 1)
        key_row = lax.broadcasted_iota(jnp.int32, (128, 1024), 0)
        own_q.wait()
        many(qbuf.at[t], NZ - 1, q_snd, q_rcv.at[t]).wait_recv()
        qs = qbuf[t].reshape(128, 128)
        scores = lax.dot_general(
            qs, kbuf[t].reshape(1024, 128), (((1,), (1,)), ((), ())), preferred_element_type=F32
        ) * (128 ** -0.5)
        valid = jnp.logical_and(
            key_lane // 64 == key_row % 16, (key_lane % 64).astype(F32) < own_len
        )
        exps = jnp.where(valid, jnp.exp(scores), 0.0)
        weights = (exps / jnp.sum(exps, axis=1, keepdims=True)).astype(BF)
        context = jnp.dot(weights, vbuf[t].reshape(1024, 128), preferred_element_type=F32)
        grid[1, t, z, y] = context.astype(BF)

        drain_c = gather(1, t, lambda zs: None)

        @pl.when(t == 0)
        def _():
            loads[2].wait()

        attended = jnp.zeros((128, 128), F32)
        for yy in range(NY):
            for h in range(0, NZ, 4):
                lhs = jnp.concatenate(
                    [grid[1, t, :, yy, 16 * hh : 16 * hh + 16, :].reshape(128, 128) for hh in range(h, h + 4)],
                    axis=1,
                )
                k0 = 128 * (yy * NZ + h)
                attended += jnp.dot(lhs, wo_v[k0 : k0 + 512, :], preferred_element_type=F32)
        middle = grid[0, t, z, y].astype(F32) + attended
        mid[...] = middle
        grid[2, t, z, y] = middle.astype(BF)

        @pl.when(t == 0)
        def _():
            for c in loads[3:7]:
                c.wait()

        acc[...] = jnp.zeros_like(acc)

        def take_ffn(zs):
            total, lhs = scaled_block(2, t, gf_v, zs)
            acc[:, 0:768] += jnp.dot(lhs, weight_rows(wgu_v, zs), preferred_element_type=F32)
            acc[:, 768:896] += jnp.broadcast_to(total, (128, 128))

        drain_d = gather(2, t, take_ffn)
        scale = lax.rsqrt(acc[:, 768:769] / d_model + EPS)
        share = meta_column(t * 16 + e // 2)
        gate = acc[:, 0:384] * scale
        upv = acc[:, 384:768] * scale
        act[...] = (gate / (1.0 + jnp.exp(-gate)) * upv * share).astype(BF)

        def to(d):
            return (z + d) % NZ

        def rh_copy(d, way):
            dst = up if way == 0 else down
            return remote(
                part.at[t, to(d), far, pl.ds(64 * way, 64)], half_in.at[t, to(d), way],
                rh_send.at[d, way], rh_recv.at[t, d, way], dev(dst, z),
            )

        def rf_copy(d, way):
            dst = up if way == 0 else down
            return remote(
                full_out.at[t, to(d), way], full_in.at[t, to(d), way],
                rf_send.at[d, way], rf_recv.at[t, d, way], dev(dst, z),
            )

        def rz_copy(d):
            return remote(ysum.at[t, to(d)], zin.at[t, d], rz_send.at[d], rz_recv.at[t, d], dev(y, to(d)))

        for k in range(NZ + 2):
            if k < NZ:
                d = FAR_FIRST[k]
                w = jnp.concatenate(
                    [wd_v[:, pl.ds(column_start(to(d), yy), 128)] for yy in range(NY)], axis=1
                )
                res = jnp.dot(act[...], w, preferred_element_type=F32).astype(BF)
                for yy in range(NY):
                    part[t, to(d), yy] = res[:, 128 * yy : 128 * yy + 128]
                rh_copy(d, 0).start()
                rh_copy(d, 1).start()
            if 1 <= k <= NZ:
                d = FAR_FIRST[k - 1]
                for way in range(2):
                    rh_copy(d, way).wait_recv()
                    dst = up if way == 0 else down
                    lo, hi = 64 * way, 64 * (1 - way)
                    full_out[t, to(d), way, lo : lo + 64, :] = (
                        part[t, to(d), dst, lo : lo + 64, :].astype(F32) + half_in[t, to(d), way].astype(F32)
                    ).astype(BF)
                    full_out[t, to(d), way, hi : hi + 64, :] = part[t, to(d), dst, hi : hi + 64, :]
                    rf_copy(d, way).start()
            if k >= 2:
                d = FAR_FIRST[k - 2]
                for way in range(2):
                    rf_copy(d, way).wait_recv()
                total = (
                    part[t, to(d), y].astype(F32)
                    + full_in[t, to(d), 0].astype(F32)
                    + full_in[t, to(d), 1].astype(F32)
                )
                if d:
                    ysum[t, to(d)] = total.astype(BF)
                    rz_copy(d).start()
                else:
                    mid[...] += total
        result = mid[...]
        for d in (7, 1, 6, 2, 5, 3, 4):
            rz_copy(d).wait_recv()
            result = result + zin[t, d].astype(F32)
        rows[...] = result

        @pl.when(t < STEPS - 1)
        def _():
            hop = remote(
                grid.at[3, t, z, y], grid.at[0, t + 1, z, y], hop_send.at[t + 1], hop_recv.at[t + 1],
                {"section": nxt},
            )
            grid[3, t, z, y] = result.astype(BF)
            hop.start()
            hop.wait_send()

        drain_a()
        drain_c()
        drain_d()
        many(qbuf.at[t], NZ - 1, q_snd, q_rcv.at[t]).wait_send()
        for d in FAR_FIRST:
            for way in range(2):
                rh_copy(d, way).wait_send()
                rf_copy(d, way).wait_send()
            if d:
                rz_copy(d).wait_send()
        return carry

    lax.fori_loop(0, STEPS, step, 0)

    for i in range(n):
        osend[i] = rows[4 * i : 4 * i + 4, :].astype(BF)

    def o_copy(d):
        p = (e + d) % n
        return remote(
            osend.at[(p % NZ) * NY + p // NZ], obuf.at[e], o_sem.at[0], o_sem.at[1], {"expert": p}
        )

    def send_out(d, _):
        o_copy(d).start()
        return 0

    lax.fori_loop(1, n, send_out, 0)
    own_o = pltpu.make_async_copy(osend.at[z * NY + y], obuf.at[e], o_sem.at[2])
    own_o.start()
    for t in range(STEPS):
        for d in range(1, NY):
            for c in kv_copies(t, d):
                c.wait_send()
    many(hbuf, n - 1, sm_send.at[0], sm_recv.at[0]).wait_send()
    many(mbuf, n - 1, sm_send.at[1], sm_recv.at[1]).wait_send()
    own_o.wait()
    many(obuf, n - 1, o_sem.at[0], o_sem.at[1]).wait_recv()
    for i in range(n):
        out[:, 128 * i : 128 * i + 128] = obuf[i]
    many(obuf, n - 1, o_sem.at[0], o_sem.at[1]).wait_send()


def body(
    hidden_in, attn_gain, w_query, w_out, key_cache, value_cache, lengths, ffn_gain,
    w_gate, w_up, w_down, routes, gates,
):
    experts = NY * NZ // 2
    shares = gates[0] / jnp.sum(gates[0], axis=-1, keepdims=True)
    hits = routes[0][:, :, :, None] == jnp.arange(experts, dtype=jnp.int32)
    coeffs = jnp.sum(jnp.where(hits, shares[..., None], 0.0), axis=2)
    coeffs = coeffs.transpose(1, 0, 2).reshape(4, STEPS * experts)
    meta = jnp.concatenate(
        [
            coeffs,
            jnp.zeros((4, 64 - STEPS * experts), F32),
            lengths[0].T.astype(F32),
            jnp.zeros((4, 64 - STEPS), F32),
        ],
        axis=1,
    )

    def by_head(cache):
        return cache[0].transpose(3, 0, 1, 2, 4).reshape(NY, STEPS, 256, 128)

    DMA = pltpu.SemaphoreType.DMA
    V = pltpu.VMEM
    scratch = [
        V((4096, 128), BF), V((4096, 128), BF), V((4096, 768), BF), V((384, 4096), BF),
        V((1, 4096), BF), V((1, 4096), BF),
        V((STEPS, NY, 256, 128), BF), V((STEPS, NY, 256, 128), BF),
        V((32, 4, 128), BF), V((32, 4, 128), F32), V((128, 128), F32), V((128, 128), F32),
        V((4, STEPS, NZ, NY, 128, 128), BF),
        V((STEPS, NZ, 16, 128), BF), V((STEPS, NZ, 16, 128), BF),
        V((STEPS, NZ, NY, 128, 128), BF),
        V((STEPS, NZ, 2, 64, 128), BF),
        V((STEPS, NZ, 2, 128, 128), BF), V((STEPS, NZ, 2, 128, 128), BF),
        V((STEPS, NZ, 128, 128), BF), V((STEPS, NZ, 128, 128), BF),
        V((128, 128), F32), V((128, 896), F32), V((128, 384), BF),
        V((32, 4, 128), BF), V((32, 4, 128), BF),
        DMA((7,)), DMA((2, STEPS)), DMA((2, STEPS, NY)), DMA((2, STEPS, NY)),
        DMA((2,)), DMA((2,)), DMA((2,)),
        DMA((3, NZ)), DMA((3, STEPS, NZ)),
        DMA((3, NZ, 2)), DMA((3, STEPS, NZ, 2)),
        DMA((3, NZ, 2)), DMA((3, STEPS, NZ, 2)),
        DMA, DMA, DMA((STEPS,)),
        DMA((NZ, 2)), DMA((STEPS, NZ, 2)),
        DMA((NZ, 2)), DMA((STEPS, NZ, 2)),
        DMA((NZ,)), DMA((STEPS, NZ)),
        DMA((STEPS,)), DMA((STEPS,)), DMA((3,)),
    ]
    hbm = pl.BlockSpec(memory_space=pl.ANY)
    out = pl.pallas_call(
        kernel,
        out_shape=jax.ShapeDtypeStruct((4, 4096), BF),
        in_specs=[hbm] * 11,
        out_specs=pl.BlockSpec(memory_space=pltpu.VMEM),
        scratch_shapes=scratch,
        compiler_params=pltpu.CompilerParams(
            collective_id=0, has_side_effects=True, vmem_limit_bytes=60 * 1024 * 1024
        ),
        name="relay_layers",
    )(
        hidden_in[0], meta, attn_gain, ffn_gain, w_query[0], w_out[0], w_gate[0, 0], w_up[0, 0], w_down[0, 0],
        by_head(key_cache), by_head(value_cache),
    )
    return out[None]


def solution(mesh):
    return jax.shard_map(
        body,
        mesh=mesh,
        in_specs=(
            P("section", "expert", None),
            P("section", None),
            P("section", None, "expert"),
            P("section", None, "expert"),
            P("section", None, "expert", None, None, None),
            P("section", None, "expert", None, None, None),
            P("section", None, "expert"),
            P("section", None),
            P("section", "expert", None, None),
            P("section", "expert", None, None),
            P("section", "expert", None, None),
            P("section", None, "expert", None),
            P("section", None, "expert", None),
        ),
        out_specs=P("section", "expert", None),
        check_vma=False,
    )
```

```python
import jax
import jax.numpy as jnp
from jax import lax
from jax.experimental import pallas as pl
from jax.experimental.pallas import tpu as pltpu
from jax.sharding import PartitionSpec as P

STEPS = 3
NY = 4
NZ = 8
EPS = 1e-06
NEAR_FIRST = (0, 1, 7, 2, 6, 3, 5, 4)
FAR_FIRST = (4, 3, 5, 2, 6, 1, 7, 0)
BF = jnp.bfloat16
F32 = jnp.float32
MESH = pl.DeviceIdType.MESH


def remote(src, dst, send, recv, peer):
    return pltpu.make_async_remote_copy(
        src_ref=src, dst_ref=dst, send_sem=send, recv_sem=recv, device_id=peer, device_id_type=MESH
    )


def pieces_to_rows(pieces, rows):
    for i in range(pieces.shape[0]):
        rows[4 * i : 4 * i + 4, :] = pieces[i].astype(F32)


def kernel(
    hid, meta, again, fgain, wq, wo, wg, wu, wd, kt, vt,
    out,
    wq_v, wo_v, wgu_v, wd_v, ga_v, gf_v, kbuf, vbuf,
    hbuf, mbuf, rows, mrows, grid, qsend, qbuf, part, y_in, ysum, zin,
    mid, acc, act, osend, obuf,
    load_sem, kv_own, kv_send, kv_recv, sm_own, sm_send, sm_recv,
    z_send, z_recv, y_send, y_recv, f_send, f_recv,
    q_own, q_snd, q_rcv, ry_send, ry_recv, rz_send, rz_recv,
    hop_send, hop_recv, o_sem,
):
    e = lax.axis_index("expert")
    s = lax.axis_index("section")
    y, z = e // NZ, e % NZ
    nsec = lax.axis_size("section")
    n = NY * NZ
    nxt, prv = (s + 1) % nsec, (s + nsec - 1) % nsec
    up, down, far = (y + 1) % NY, (y + NY - 1) % NY, (y + 2) % NY

    def dev(yy, zz):
        return {"expert": yy * NZ + zz}

    loads = [
        pltpu.make_async_copy(wq, wq_v, load_sem.at[0]),
        pltpu.make_async_copy(again, ga_v, load_sem.at[1]),
        pltpu.make_async_copy(wo, wo_v, load_sem.at[2]),
        pltpu.make_async_copy(fgain, gf_v, load_sem.at[3]),
        pltpu.make_async_copy(wg, wgu_v.at[:, 0:384], load_sem.at[4]),
        pltpu.make_async_copy(wu, wgu_v.at[:, 384:768], load_sem.at[5]),
        pltpu.make_async_copy(wd, wd_v, load_sem.at[6]),
    ]
    for c in loads:
        c.start()

    barrier = pltpu.get_barrier_semaphore()

    def greet(d, _):
        pl.semaphore_signal(barrier, inc=1, device_id={"expert": (e + d) % n}, device_id_type=MESH)
        return 0

    lax.fori_loop(1, n, greet, 0)
    pl.semaphore_signal(barrier, inc=1, device_id={"section": nxt}, device_id_type=MESH)
    pl.semaphore_signal(barrier, inc=1, device_id={"section": prv}, device_id_type=MESH)
    pl.semaphore_wait(barrier, n + 1)

    def hid_copy(p):
        return remote(
            hid.at[:, pl.ds(pl.multiple_of(128 * p, 128), 128)], hbuf.at[z * NY + y],
            sm_send.at[0], sm_recv.at[0], {"expert": p},
        )

    def meta_copy(p):
        return remote(meta, mbuf.at[z * NY + y], sm_send.at[1], sm_recv.at[1], {"expert": p})

    def send_start(d, _):
        p = (e + d) % n
        hid_copy(p).start()
        return 0

    def send_meta(d, _):
        meta_copy((e + d) % n).start()
        return 0

    own_h = pltpu.make_async_copy(
        hid.at[:, pl.ds(pl.multiple_of(128 * e, 128), 128)], hbuf.at[z * NY + y], sm_own.at[0]
    )
    own_m = pltpu.make_async_copy(meta, mbuf.at[z * NY + y], sm_own.at[1])
    own_h.start()
    own_m.start()
    lax.fori_loop(1, n, send_start, 0)
    lax.fori_loop(1, n, send_meta, 0)

    def kv_copies(t, d):
        yy = (y + d) % NY
        return (
            remote(kt.at[yy, t], kbuf.at[t, y], kv_send.at[0, t, d], kv_recv.at[0, t, d], dev(yy, z)),
            remote(vt.at[yy, t], vbuf.at[t, y], kv_send.at[1, t, d], kv_recv.at[1, t, d], dev(yy, z)),
        )

    def kv_owns(t):
        return (
            pltpu.make_async_copy(kt.at[y, t], kbuf.at[t, y], kv_own.at[0, t]),
            pltpu.make_async_copy(vt.at[y, t], vbuf.at[t, y], kv_own.at[1, t]),
        )

    for t in range(STEPS):
        for c in kv_owns(t):
            c.start()
    for d in range(1, NY):
        for c in kv_copies(0, d):
            c.start()

    def many(ref, k, send, recv):
        view = ref.at[pl.ds(0, k)]
        return remote(view, view, send, recv, {"expert": (e + 1) % n})

    own_h.wait()
    many(hbuf, n - 1, sm_send.at[0], sm_recv.at[0]).wait_recv()
    pieces_to_rows(hbuf, rows)
    grid[0, 0, z, y] = rows[...].astype(BF)
    own_m.wait()
    many(mbuf, n - 1, sm_send.at[1], sm_recv.at[1]).wait_recv()
    pieces_to_rows(mbuf, mrows)

    def gather(g, t, consume):
        def z_copy(d):
            b = grid.at[g, t, z, y]
            return remote(b, b, z_send.at[g, d], z_recv.at[g, t, d], dev(y, (z + d) % NZ))

        def src(d):
            return (z + NZ - d) % NZ

        def y_copy(d, way):
            b = grid.at[g, t, src(d), y]
            to = up if way == 0 else down
            return remote(b, b, y_send.at[g, d, way], y_recv.at[g, t, d, way], dev(to, z))

        def f_copy(d):
            b = grid.at[g, t, src(d), y]
            return remote(b, b, f_send.at[g, d], f_recv.at[g, t, d], dev(far, z))

        def forward(d):
            y_copy(d, 0).start()
            y_copy(d, 1).start()
            f_copy(d).start()

        def take(d):
            y_copy(d, 0).wait_recv()
            y_copy(d, 1).wait_recv()
            f_copy(d).wait_recv()
            consume(src(d))

        for d in NEAR_FIRST[1:]:
            z_copy(d).start()
        forward(0)
        for d in NEAR_FIRST[1:]:
            z_copy(d).wait_recv()
            forward(d)
            if d == 6:
                take(0)
        for d in NEAR_FIRST[1:]:
            take(d)

        def drain():
            for d in NEAR_FIRST:
                if d:
                    z_copy(d).wait_send()
                y_copy(d, 0).wait_send()
                y_copy(d, 1).wait_send()
                f_copy(d).wait_send()

        return drain

    def column_start(zs, yy):
        return pl.multiple_of(128 * (yy * NZ + zs), 128)

    def scaled_block(g, t, gain_v, zs):
        xs = [grid[g, t, zs, yy].astype(F32) for yy in range(NY)]
        total = sum(jnp.sum(x * x, axis=1, keepdims=True) for x in xs)
        parts = [
            (xs[yy] * gain_v[:, pl.ds(column_start(zs, yy), 128)].astype(F32)).astype(BF) for yy in range(NY)
        ]
        return total, jnp.concatenate(parts, axis=1)

    def weight_rows(w, zs):
        return jnp.concatenate([w[pl.ds(column_start(zs, yy), 128), :] for yy in range(NY)], axis=0)

    lane = lax.broadcasted_iota(jnp.int32, (128, 128), 1)

    def meta_column(index):
        return jnp.sum(jnp.where(lane == index, mrows[...], 0.0), axis=1, keepdims=True)

    d_model = NY * NZ * 128

    def step(t, carry):
        @pl.when(t > 0)
        def _():
            b = grid.at[0, t, z, y]
            remote(b, b, hop_send.at[t], hop_recv.at[t], {"section": nxt}).wait_recv()

        @pl.when(t == 0)
        def _():
            for c in loads[0:2]:
                c.wait()

        sums = jnp.zeros((128, 1), F32)
        acc[:, 0:128] = jnp.zeros((128, 128), F32)
        acc[:, 128:256] = jnp.zeros((128, 128), F32)

        def take_query(zs):
            total, lhs = scaled_block(0, t, ga_v, zs)
            acc[:, 0:128] += jnp.dot(lhs, weight_rows(wq_v, zs), preferred_element_type=F32)
            acc[:, 128:256] += jnp.broadcast_to(total, (128, 128))

        drain_a = gather(0, t, take_query)
        scale = lax.rsqrt(acc[:, 128:256] / d_model + EPS)
        query = acc[:, 0:128] * scale
        query = query * lax.rsqrt(jnp.mean(query * query, axis=1, keepdims=True) + EPS)
        qsend[t] = query.astype(BF).reshape(NZ, 16, 128)

        def q_copy(d):
            zz = (z + d) % NZ
            return remote(qsend.at[t, zz], qbuf.at[t, z], q_snd, q_rcv.at[t], dev(y, zz))

        own_q = pltpu.make_async_copy(qsend.at[t, z], qbuf.at[t, z], q_own)
        own_q.start()
        for d in NEAR_FIRST[1:]:
            q_copy(d).start()

        @pl.when(t < STEPS - 1)
        def _():
            for d in range(1, NY):
                for c in kv_copies(t + 1, d):
                    c.start()

        for c in kv_owns(t):
            c.wait()
        for d in range(1, NY):
            for c in kv_copies(t, d):
                c.wait_recv()
        length = meta_column(64 + t)
        pos = lax.broadcasted_iota(jnp.int32, (128, 128), 0)
        pick = jnp.where(lane == z * 16 + pos % 16, 1.0, 0.0)
        own_len = jnp.dot(pick, length * jnp.ones((1, 128), F32), precision=lax.Precision.HIGHEST)[:, 0:1]
        key_lane = lax.broadcasted_iota(jnp.int32, (128, 1024), 1)
        key_row = lax.broadcasted_iota(jnp.int32, (128, 1024), 0)
        own_q.wait()
        many(qbuf.at[t], NZ - 1, q_snd, q_rcv.at[t]).wait_recv()
        qs = qbuf[t].reshape(128, 128)
        scores = lax.dot_general(
            qs, kbuf[t].reshape(1024, 128), (((1,), (1,)), ((), ())), preferred_element_type=F32
        ) * (128 ** -0.5)
        valid = jnp.logical_and(
            key_lane // 64 == key_row % 16, (key_lane % 64).astype(F32) < own_len
        )
        exps = jnp.where(valid, jnp.exp(scores), 0.0)
        weights = (exps / jnp.sum(exps, axis=1, keepdims=True)).astype(BF)
        context = jnp.dot(weights, vbuf[t].reshape(1024, 128), preferred_element_type=F32)
        grid[1, t, z, y] = context.astype(BF)

        drain_c = gather(1, t, lambda zs: None)

        @pl.when(t == 0)
        def _():
            loads[2].wait()

        attended = jnp.zeros((128, 128), F32)
        for yy in range(NY):
            for h in range(0, NZ, 4):
                lhs = jnp.concatenate(
                    [grid[1, t, :, yy, 16 * hh : 16 * hh + 16, :].reshape(128, 128) for hh in range(h, h + 4)],
                    axis=1,
                )
                k0 = 128 * (yy * NZ + h)
                attended += jnp.dot(lhs, wo_v[k0 : k0 + 512, :], preferred_element_type=F32)
        middle = grid[0, t, z, y].astype(F32) + attended
        mid[...] = middle
        grid[2, t, z, y] = middle.astype(BF)

        @pl.when(t == 0)
        def _():
            for c in loads[3:7]:
                c.wait()

        acc[...] = jnp.zeros_like(acc)

        def take_ffn(zs):
            total, lhs = scaled_block(2, t, gf_v, zs)
            acc[:, 0:768] += jnp.dot(lhs, weight_rows(wgu_v, zs), preferred_element_type=F32)
            acc[:, 768:896] += jnp.broadcast_to(total, (128, 128))

        drain_d = gather(2, t, take_ffn)
        scale = lax.rsqrt(acc[:, 768:769] / d_model + EPS)
        share = meta_column(t * 16 + e // 2)
        gate = acc[:, 0:384] * scale
        upv = acc[:, 384:768] * scale
        act[...] = (gate / (1.0 + jnp.exp(-gate)) * upv * share).astype(BF)

        def to(d):
            return (z + d) % NZ

        def ry_copy(d, way):
            peer = (up, down, far)[way]
            return remote(
                part.at[t, to(d), peer], y_in.at[t, to(d), way],
                ry_send.at[d, way], ry_recv.at[t, d, way], dev(peer, z),
            )

        def rz_copy(d):
            return remote(ysum.at[t, to(d)], zin.at[t, d], rz_send.at[d], rz_recv.at[t, d], dev(y, to(d)))

        for d in FAR_FIRST:
            w = jnp.concatenate(
                [wd_v[:, pl.ds(column_start(to(d), yy), 128)] for yy in range(NY)], axis=1
            )
            res = jnp.dot(act[...], w, preferred_element_type=F32).astype(BF)
            for yy in range(NY):
                part[t, to(d), yy] = res[:, 128 * yy : 128 * yy + 128]
            for way in range(3):
                ry_copy(d, way).start()
        for d in FAR_FIRST:
            total = part[t, to(d), y].astype(F32)
            for way in range(3):
                ry_copy(d, way).wait_recv()
                total = total + y_in[t, to(d), way].astype(F32)
            if d:
                ysum[t, to(d)] = total.astype(BF)
                rz_copy(d).start()
            else:
                mid[...] += total
        result = mid[...]
        for d in (7, 1, 6, 2, 5, 3, 4):
            rz_copy(d).wait_recv()
            result = result + zin[t, d].astype(F32)
        rows[...] = result

        @pl.when(t < STEPS - 1)
        def _():
            hop = remote(
                grid.at[3, t, z, y], grid.at[0, t + 1, z, y], hop_send.at[t + 1], hop_recv.at[t + 1],
                {"section": nxt},
            )
            grid[3, t, z, y] = result.astype(BF)
            hop.start()
            hop.wait_send()

        drain_a()
        drain_c()
        drain_d()
        many(qbuf.at[t], NZ - 1, q_snd, q_rcv.at[t]).wait_send()
        for d in FAR_FIRST:
            for way in range(3):
                ry_copy(d, way).wait_send()
            if d:
                rz_copy(d).wait_send()
        return carry

    lax.fori_loop(0, STEPS, step, 0)

    for i in range(n):
        osend[i] = rows[4 * i : 4 * i + 4, :].astype(BF)

    def o_copy(d):
        p = (e + d) % n
        return remote(
            osend.at[(p % NZ) * NY + p // NZ], obuf.at[e], o_sem.at[0], o_sem.at[1], {"expert": p}
        )

    def send_out(d, _):
        o_copy(d).start()
        return 0

    lax.fori_loop(1, n, send_out, 0)
    own_o = pltpu.make_async_copy(osend.at[z * NY + y], obuf.at[e], o_sem.at[2])
    own_o.start()
    for t in range(STEPS):
        for d in range(1, NY):
            for c in kv_copies(t, d):
                c.wait_send()
    many(hbuf, n - 1, sm_send.at[0], sm_recv.at[0]).wait_send()
    many(mbuf, n - 1, sm_send.at[1], sm_recv.at[1]).wait_send()
    own_o.wait()
    many(obuf, n - 1, o_sem.at[0], o_sem.at[1]).wait_recv()
    for i in range(n):
        out[:, 128 * i : 128 * i + 128] = obuf[i]
    many(obuf, n - 1, o_sem.at[0], o_sem.at[1]).wait_send()


def body(
    hidden_in, attn_gain, w_query, w_out, key_cache, value_cache, lengths, ffn_gain,
    w_gate, w_up, w_down, routes, gates,
):
    experts = NY * NZ // 2
    shares = gates[0] / jnp.sum(gates[0], axis=-1, keepdims=True)
    hits = routes[0][:, :, :, None] == jnp.arange(experts, dtype=jnp.int32)
    coeffs = jnp.sum(jnp.where(hits, shares[..., None], 0.0), axis=2)
    coeffs = coeffs.transpose(1, 0, 2).reshape(4, STEPS * experts)
    meta = jnp.concatenate(
        [
            coeffs,
            jnp.zeros((4, 64 - STEPS * experts), F32),
            lengths[0].T.astype(F32),
            jnp.zeros((4, 64 - STEPS), F32),
        ],
        axis=1,
    )

    def by_head(cache):
        return cache[0].transpose(3, 0, 1, 2, 4).reshape(NY, STEPS, 256, 128)

    DMA = pltpu.SemaphoreType.DMA
    V = pltpu.VMEM
    scratch = [
        V((4096, 128), BF), V((4096, 128), BF), V((4096, 768), BF), V((384, 4096), BF),
        V((1, 4096), BF), V((1, 4096), BF),
        V((STEPS, NY, 256, 128), BF), V((STEPS, NY, 256, 128), BF),
        V((32, 4, 128), BF), V((32, 4, 128), F32), V((128, 128), F32), V((128, 128), F32),
        V((4, STEPS, NZ, NY, 128, 128), BF),
        V((STEPS, NZ, 16, 128), BF), V((STEPS, NZ, 16, 128), BF),
        V((STEPS, NZ, NY, 128, 128), BF),
        V((STEPS, NZ, 3, 128, 128), BF),
        V((STEPS, NZ, 128, 128), BF), V((STEPS, NZ, 128, 128), BF),
        V((128, 128), F32), V((128, 896), F32), V((128, 384), BF),
        V((32, 4, 128), BF), V((32, 4, 128), BF),
        DMA((7,)), DMA((2, STEPS)), DMA((2, STEPS, NY)), DMA((2, STEPS, NY)),
        DMA((2,)), DMA((2,)), DMA((2,)),
        DMA((3, NZ)), DMA((3, STEPS, NZ)),
        DMA((3, NZ, 2)), DMA((3, STEPS, NZ, 2)),
        DMA((3, NZ)), DMA((3, STEPS, NZ)),
        DMA, DMA, DMA((STEPS,)),
        DMA((NZ, 3)), DMA((STEPS, NZ, 3)),
        DMA((NZ,)), DMA((STEPS, NZ)),
        DMA((STEPS,)), DMA((STEPS,)), DMA((3,)),
    ]
    hbm = pl.BlockSpec(memory_space=pl.ANY)
    out = pl.pallas_call(
        kernel,
        out_shape=jax.ShapeDtypeStruct((4, 4096), BF),
        in_specs=[hbm] * 11,
        out_specs=pl.BlockSpec(memory_space=pltpu.VMEM),
        scratch_shapes=scratch,
        compiler_params=pltpu.CompilerParams(
            collective_id=0, has_side_effects=True, vmem_limit_bytes=60 * 1024 * 1024
        ),
        name="relay_layers",
    )(
        hidden_in[0], meta, attn_gain, ffn_gain, w_query[0], w_out[0], w_gate[0, 0], w_up[0, 0], w_down[0, 0],
        by_head(key_cache), by_head(value_cache),
    )
    return out[None]


def solution(mesh):
    return jax.shard_map(
        body,
        mesh=mesh,
        in_specs=(
            P("section", "expert", None),
            P("section", None),
            P("section", None, "expert"),
            P("section", None, "expert"),
            P("section", None, "expert", None, None, None),
            P("section", None, "expert", None, None, None),
            P("section", None, "expert"),
            P("section", None),
            P("section", "expert", None, None),
            P("section", "expert", None, None),
            P("section", "expert", None, None),
            P("section", None, "expert", None),
            P("section", None, "expert", None),
        ),
        out_specs=P("section", "expert", None),
        check_vma=False,
    )
```

```python
import jax
import jax.numpy as jnp
from jax import lax
from jax.experimental import pallas as pl
from jax.experimental.pallas import tpu as pltpu
from jax.sharding import PartitionSpec as P

STEPS = 3
NY = 4
NZ = 8
EPS = 1e-06
NEAR_FIRST = (0, 1, 7, 2, 6, 3, 5, 4)
FAR_FIRST = (4, 3, 5, 2, 6, 1, 7, 0)
BF = jnp.bfloat16
F32 = jnp.float32
MESH = pl.DeviceIdType.MESH


def remote(src, dst, send, recv, peer):
    return pltpu.make_async_remote_copy(
        src_ref=src, dst_ref=dst, send_sem=send, recv_sem=recv, device_id=peer, device_id_type=MESH
    )


def pieces_to_rows(pieces, rows):
    for i in range(pieces.shape[0]):
        rows[4 * i : 4 * i + 4, :] = pieces[i].astype(F32)


def kernel(
    hid, routes, gates, lens, again, fgain, wq, wo, wg, wu, wd, kt, vt,
    out,
    wq_v, wo_v, wgu_v, wd_v, ga_v, gf_v, kbuf, vbuf,
    r_v, g_v, l_v, meta, hbuf, mbuf, rows, mrows, xg, ctx, grid, qsend, qbuf, ssend, sbuf, opart, o_in, part, y_in, ysum, zin,
    mid, acc, act, osend, obuf,
    load_sem, w_send, w_recv, kv_own, kv_send, kv_recv, sm_own, sm_send, sm_recv,
    z_send, z_recv, y_send, y_recv,
    q_own, q_snd, q_rcv, s_snd, s_rcv, ao_send, ao_recv, ry_send, ry_recv, rz_send, rz_recv,
    o_sem,
):
    e = lax.axis_index("expert")
    s = lax.axis_index("section")
    y, z = e // NZ, e % NZ
    nsec = lax.axis_size("section")
    n = NY * NZ
    nxt, prv = (s + 1) % nsec, (s + nsec - 1) % nsec
    up, down, far = (y + 1) % NY, (y + NY - 1) % NY, (y + 2) % NY
    d_model = n * 128
    H = 64

    def dev(yy, zz):
        return {"expert": yy * NZ + zz}

    def place(yy, zz):
        return (yy // 2) * 16 + zz * 2 + yy % 2

    loads = [
        pltpu.make_async_copy(again, ga_v, load_sem.at[0]),
        pltpu.make_async_copy(fgain, gf_v, load_sem.at[1]),
        pltpu.make_async_copy(wg, wgu_v.at[:, 0:384], load_sem.at[2]),
        pltpu.make_async_copy(wu, wgu_v.at[:, 384:768], load_sem.at[3]),
        pltpu.make_async_copy(wd, wd_v, load_sem.at[4]),
        pltpu.make_async_copy(routes, r_v, load_sem.at[7]),
        pltpu.make_async_copy(gates, g_v, load_sem.at[8]),
        pltpu.make_async_copy(lens, l_v, load_sem.at[9]),
    ]

    def quarter(w, w_v, yy):
        return (
            w.at[pl.ds(pl.multiple_of(1024 * yy, 1024), 1024), :],
            w_v.at[:, pl.ds(pl.multiple_of(128 * y, 128), 128)],
        )

    def own_weight(i):
        return pltpu.make_async_copy(*quarter((wq, wo)[i], (wq_v, wo_v)[i], y), load_sem.at[5 + i])

    def weight_copy(i, d):
        yy = (y + d) % NY
        return remote(
            *quarter((wq, wo)[i], (wq_v, wo_v)[i], yy), w_send.at[i, d], w_recv.at[i, d], dev(yy, z)
        )

    for c in loads[5:8]:
        c.start()
    own_weight(0).start()
    own_weight(1).start()
    for c in loads[0:5]:
        c.start()

    barrier = pltpu.get_barrier_semaphore()

    def greet(d, _):
        pl.semaphore_signal(barrier, inc=1, device_id={"expert": (e + d) % n}, device_id_type=MESH)
        return 0

    lax.fori_loop(1, n, greet, 0)

    def greet_section(zz, _):
        for sec in (nxt, prv):
            pl.semaphore_signal(
                barrier, inc=1, device_id={"section": sec, "expert": y * NZ + zz}, device_id_type=MESH
            )
        return 0

    lax.fori_loop(0, NZ, greet_section, 0)

    for c in loads[5:8]:
        c.wait()
    slot = lax.broadcasted_iota(jnp.int32, (4, 128), 1)
    eye = lax.broadcasted_iota(jnp.int32, (4, 4), 0) == lax.broadcasted_iota(jnp.int32, (4, 4), 1)
    table = jnp.zeros((4, 128), F32)
    for t in range(STEPS):
        share = g_v[t] / jnp.sum(g_v[t], axis=1, keepdims=True)
        for k in range(8):
            table = table + jnp.where(slot == r_v[t][:, k : k + 1] + 16 * t, share[:, k : k + 1], 0.0)
        length = jnp.sum(jnp.where(eye, l_v[t : t + 1, :].astype(F32), 0.0), axis=1, keepdims=True)
        table = table + jnp.where(slot == 64 + t, length, 0.0)
    meta[...] = table
    pl.semaphore_wait(barrier, n - 1 + 2 * NZ)

    mine = place(y, z)

    def hid_copy(p):
        return remote(
            hid.at[:, pl.ds(pl.multiple_of(128 * p, 128), 128)], hbuf.at[mine],
            sm_send.at[0], sm_recv.at[0], {"expert": p},
        )

    def meta_copy(p):
        return remote(meta, mbuf.at[mine], sm_send.at[1], sm_recv.at[1], {"expert": p})

    def send_start(d, _):
        hid_copy((e + d) % n).start()
        return 0

    def send_meta(d, _):
        meta_copy((e + d) % n).start()
        return 0

    own_h = pltpu.make_async_copy(
        hid.at[:, pl.ds(pl.multiple_of(128 * e, 128), 128)], hbuf.at[mine], sm_own.at[0]
    )
    own_m = pltpu.make_async_copy(meta, mbuf.at[mine], sm_own.at[1])
    own_h.start()
    own_m.start()
    lax.fori_loop(1, n, send_start, 0)

    def kv_copies(t, d):
        yy = (y + d) % NY
        return (
            remote(kt.at[yy, t], kbuf.at[t, y], kv_send.at[0, t, d], kv_recv.at[0, t, d], dev(yy, z)),
            remote(vt.at[yy, t], vbuf.at[t, y], kv_send.at[1, t, d], kv_recv.at[1, t, d], dev(yy, z)),
        )

    def kv_owns(t):
        return (
            pltpu.make_async_copy(kt.at[y, t], kbuf.at[t, y], kv_own.at[0, t]),
            pltpu.make_async_copy(vt.at[y, t], vbuf.at[t, y], kv_own.at[1, t]),
        )

    for t in range(STEPS):
        for c in kv_owns(t):
            c.start()
    for d in range(1, NY):
        weight_copy(0, d).start()
    for d in range(1, NY):
        for c in kv_copies(0, d):
            c.start()
    lax.fori_loop(1, n, send_meta, 0)

    def many(ref, k, send, recv):
        view = ref.at[pl.ds(0, k)]
        return remote(view, view, send, recv, {"expert": (e + 1) % n})

    own_h.wait()
    many(hbuf, n - 1, sm_send.at[0], sm_recv.at[0]).wait_recv()
    pieces_to_rows(hbuf, rows)
    for h in range(2):
        xg[0, h, z] = rows[H * h : H * h + H, :].astype(BF)

    def from_z(d):
        return (z + NZ - d) % NZ

    class RowGather:
        def __init__(self, g, t, h, buf):
            self.g, self.t, self.h, self.buf = g, t, h, buf

        def z_copy(self, d):
            b = self.buf.at[self.t, self.h, z]
            return remote(
                b, b, z_send.at[self.g, self.h, d], z_recv.at[self.g, self.t, self.h, d], dev(y, to(d))
            )

        def issue(self):
            for d in NEAR_FIRST[1:]:
                self.z_copy(d).start()

        def take(self):
            for d in NEAR_FIRST[1:]:
                self.z_copy(d).wait_recv()

        def drain(self):
            for d in NEAR_FIRST[1:]:
                self.z_copy(d).wait_send()

    class Gather:
        GROUPS = ((0, 1), (1, 5), (5, 8))

        def __init__(self, t, h):
            self.t, self.h = t, h

        def z_copy(self, k):
            return remote(
                grid.at[self.t, self.h, y, 0], grid.at[self.t, self.h, y, k],
                z_send.at[2, self.h, k], z_recv.at[2, self.t, self.h, k], dev(y, to(NEAR_FIRST[k])),
            )

        def y_copy(self, i, way):
            first, last = self.GROUPS[i]
            b = grid.at[self.t, self.h, y, pl.ds(first, last - first)]
            return remote(
                b, b, y_send.at[self.h, i, way], y_recv.at[self.t, self.h, i, way], dev((up, down, far)[way], z)
            )

        def forward_group(self, i):
            for way in range(3):
                self.y_copy(i, way).start()

        def issue(self):
            for k in range(1, NZ):
                self.z_copy(k).start()
            self.forward_group(0)

        def forward(self):
            for i in range(1, 3):
                for k in range(*self.GROUPS[i]):
                    self.z_copy(k).wait_recv()
                self.forward_group(i)

        def take(self, consume):
            for i in range(3):
                for way in range(3):
                    self.y_copy(i, way).wait_recv()
                for k in range(*self.GROUPS[i]):
                    consume(k)

        def drain(self):
            for k in range(1, NZ):
                self.z_copy(k).wait_send()
            for i in range(3):
                for way in range(3):
                    self.y_copy(i, way).wait_send()

    def column_start(zs, yy):
        return pl.multiple_of(128 * (yy * NZ + zs), 128)

    def scaled(xs, gains):
        xs = [x.astype(F32) for x in xs]
        total = sum(jnp.sum(x * x, axis=1, keepdims=True) for x in xs)
        return total, jnp.concatenate([(x * g.astype(F32)).astype(BF) for x, g in zip(xs, gains)], axis=1)

    def weight_rows(w, zs):
        return jnp.concatenate([w[pl.ds(column_start(zs, yy), 128), :] for yy in range(NY)], axis=0)

    def lane_of(values, index):
        lane = lax.broadcasted_iota(jnp.int32, values.shape, 1)
        return jnp.sum(jnp.where(lane == index, values, 0.0), axis=1, keepdims=True)

    def to(d):
        return (z + d) % NZ

    def q_copy(t, h, d):
        p = (e + d) % n
        return remote(qsend.at[t, h, p], qbuf.at[t, h, e], q_snd.at[h], q_rcv.at[t, h], {"expert": p})

    def s_copy(t, h, d):
        yy = (y + d) % NY
        return remote(ssend.at[t, h], sbuf.at[t, h, y], s_snd.at[h, d], s_rcv.at[t, h, d], dev(yy, z))

    def ao_copy(t, h, way):
        peer = (up, down, far)[way]
        return remote(
            opart.at[t, h, peer], o_in.at[t, h, way], ao_send.at[h, way], ao_recv.at[t, h, way], dev(peer, z)
        )

    def ry_copy(t, h, i, way):
        peer = (up, down, far)[way]
        ks = pl.ds(4 * i, 4)
        return remote(
            part.at[t, h, peer, ks], y_in.at[t, h, way, ks],
            ry_send.at[h, i, way], ry_recv.at[t, h, i, way], dev(peer, z),
        )

    def rz_copy(t, h, k, sec):
        return remote(
            ysum.at[t, h, k], zin.at[t, h, k], rz_send.at[h, k], rz_recv.at[t, h, k],
            {"section": sec, "expert": y * NZ + to(FAR_FIRST[k])},
        )

    def layer(t, h):
        ga, gc, gd = RowGather(0, t, h, xg), RowGather(1, t, h, ctx), Gather(t, h)

        @pl.when(t > 0)
        def _():
            state = jnp.zeros((H, 128), F32)
            for k in range(NZ):
                rz_copy(t - 1, h, k, nxt).wait_recv()
                state = state + zin[t - 1, h, k].astype(F32)
            xg[t, h, z] = state.astype(BF)

        ga.issue()
        yield

        ga.take()
        if h == 0:
            @pl.when(t == 0)
            def _():
                loads[0].wait()
                own_weight(0).wait()
                for d in range(1, NY):
                    weight_copy(0, d).wait_recv()

        total, lhs = scaled(
            [xg[t, h, zz] for zz in range(NZ)],
            [ga_v[:, pl.ds(column_start(zz, y), 128)] for zz in range(NZ)],
        )
        query = jnp.dot(lhs, wq_v[...], preferred_element_type=F32)
        for yy in range(NY):
            qsend[t, h, NZ * yy : NZ * yy + NZ] = query[:, 128 * yy : 128 * yy + 128].reshape(NZ, 8, 128).astype(BF)
        acc[h, :, 0:128] = jnp.broadcast_to(total, (H, 128))
        ssend[t, h] = acc[h, pl.ds(pl.multiple_of(8 * z, 8), 8), 0:128]
        own_q = pltpu.make_async_copy(qsend.at[t, h, e], qbuf.at[t, h, e], q_own.at[h, 0])
        own_s = pltpu.make_async_copy(ssend.at[t, h], sbuf.at[t, h, y], q_own.at[h, 1])
        own_q.start()
        own_s.start()

        def send_q(d, _):
            q_copy(t, h, d).start()
            return 0

        lax.fori_loop(1, n, send_q, 0)
        for d in range(1, NY):
            s_copy(t, h, d).start()

        if h == 1:
            @pl.when(t == 0)
            def _():
                for d in range(1, NY):
                    weight_copy(1, d).start()
        yield

        if h == 0:
            for c in kv_owns(t):
                c.wait()
            for d in range(1, NY):
                for c in kv_copies(t, d):
                    c.wait_recv()

            @pl.when(t == 0)
            def _():
                own_m.wait()
                many(mbuf, n - 1, sm_send.at[1], sm_recv.at[1]).wait_recv()
                pieces_to_rows(mbuf, mrows)

        length = lane_of(mrows[pl.ds(pl.multiple_of(H * h + 8 * z, 8), 8), :], 64 + t)
        length = jnp.concatenate([length] * NZ, axis=0)
        key_lane = lax.broadcasted_iota(jnp.int32, (H, 512), 1)
        key_row = lax.broadcasted_iota(jnp.int32, (H, 512), 0)
        own_q.wait()
        own_s.wait()
        many(qbuf.at[t, h], n - 1, q_snd.at[h], q_rcv.at[t, h]).wait_recv()
        for d in range(1, NY):
            s_copy(t, h, d).wait_recv()
        query = sum(qbuf[t, h, NZ * yy : NZ * yy + NZ].astype(F32) for yy in range(NY))
        mean_x = sum(sbuf[t, h, yy] for yy in range(NY)) / d_model
        mean_q = jnp.mean(query * query, axis=2, keepdims=True)
        query = query * lax.rsqrt(mean_q + EPS * (mean_x[None] + EPS))
        qs = query.reshape(H, 128).astype(BF)
        scores = lax.dot_general(
            qs, kbuf[t, 2 * h : 2 * h + 2].reshape(512, 128), (((1,), (1,)), ((), ())),
            preferred_element_type=F32,
        ) * (128 ** -0.5)
        valid = jnp.logical_and(key_lane // 64 == key_row % 8, (key_lane % 64).astype(F32) < length)
        exps = jnp.where(valid, jnp.exp(scores), 0.0)
        weights = (exps / jnp.sum(exps, axis=1, keepdims=True)).astype(BF)
        context = jnp.dot(weights, vbuf[t, 2 * h : 2 * h + 2].reshape(512, 128), preferred_element_type=F32)
        ctx[t, h, z] = context.reshape(NZ, 8, 128).astype(BF)
        gc.issue()
        yield

        gc.take()
        if h == 0:
            @pl.when(t == 0)
            def _():
                own_weight(1).wait()
                for d in range(1, NY):
                    weight_copy(1, d).wait_recv()

        lhs = jnp.concatenate(
            [ctx[t, h, :, hh].astype(F32).reshape(H, 128).astype(BF) for hh in range(NZ)], axis=1
        )
        attended = jnp.dot(lhs, wo_v[...], preferred_element_type=F32)
        for yy in range(NY):
            opart[t, h, yy] = attended[:, 128 * yy : 128 * yy + 128].astype(BF)
        for way in range(3):
            ao_copy(t, h, way).start()
        yield
        middle = xg[t, h, z].astype(F32) + opart[t, h, y].astype(F32)
        for way in range(3):
            ao_copy(t, h, way).wait_recv()
            middle = middle + o_in[t, h, way].astype(F32)
        mid[h] = middle
        grid[t, h, y, 0] = middle.astype(BF)
        gd.issue()
        yield
        gd.forward()
        yield
        if h == 0:
            @pl.when(t == 0)
            def _():
                for c in loads[1:5]:
                    c.wait()

        acc[h] = jnp.zeros((H, 896), F32)

        def take_ffn(k):
            zs = from_z(NEAR_FIRST[k])
            total, lhs = scaled(
                [grid[t, h, yy, k] for yy in range(NY)],
                [gf_v[:, pl.ds(column_start(zs, yy), 128)] for yy in range(NY)],
            )
            acc[h, :, 0:768] += jnp.dot(lhs, weight_rows(wgu_v, zs), preferred_element_type=F32)
            acc[h, :, 768:896] += jnp.broadcast_to(total, (H, 128))

        gd.take(take_ffn)
        scale = lax.rsqrt(acc[h, :, 768:769] / d_model + EPS)
        share = lane_of(mrows[H * h : H * h + H, :], t * 16 + e // 2)
        gate = acc[h, :, 0:384] * scale
        upv = acc[h, :, 384:768] * scale
        act[h] = (gate / (1.0 + jnp.exp(-gate)) * upv * share).astype(BF)

        for i in range(2):
            for k in range(4 * i, 4 * i + 4):
                zs = to(FAR_FIRST[k])
                w = jnp.concatenate([wd_v[:, pl.ds(column_start(zs, yy), 128)] for yy in range(NY)], axis=1)
                res = jnp.dot(act[h], w, preferred_element_type=F32).astype(BF)
                for yy in range(NY):
                    part[t, h, yy, k] = res[:, 128 * yy : 128 * yy + 128]
            for way in range(3):
                ry_copy(t, h, i, way).start()
        yield
        for i in range(2):
            for way in range(3):
                ry_copy(t, h, i, way).wait_recv()
            for k in range(4 * i, 4 * i + 4):
                total = part[t, h, y, k].astype(F32)
                for way in range(3):
                    total = total + y_in[t, h, way, k].astype(F32)
                if k == NZ - 1:
                    total = total + mid[h]
                    mid[h] = total
                ysum[t, h, k] = total.astype(BF)

                @pl.when(t < STEPS - 1)
                def _():
                    rz_copy(t, h, k, nxt).start()

                if k < NZ - 1:
                    @pl.when(t == STEPS - 1)
                    def _():
                        rz_copy(t, h, k, s).start()
        if h == 1:
            @pl.when(t < STEPS - 1)
            def _():
                for d in range(1, NY):
                    for c in kv_copies(t + 1, d):
                        c.start()
        yield

        @pl.when(t == STEPS - 1)
        def _():
            result = mid[h]
            for k in range(NZ - 1):
                rz_copy(t, h, k, s).wait_recv()
                result = result + zin[t, h, k].astype(F32)
            rows[H * h : H * h + H, :] = result

        yield
        ga.drain()
        gc.drain()
        gd.drain()
        many(qbuf.at[t, h], n - 1, q_snd.at[h], q_rcv.at[t, h]).wait_send()
        for d in range(1, NY):
            s_copy(t, h, d).wait_send()
        for way in range(3):
            ao_copy(t, h, way).wait_send()
        for i in range(2):
            for way in range(3):
                ry_copy(t, h, i, way).wait_send()
        for k in range(NZ - 1):
            rz_copy(t, h, k, nxt).wait_send()

        @pl.when(t < STEPS - 1)
        def _():
            rz_copy(t, h, NZ - 1, nxt).wait_send()

    def step(t, carry):
        turns = [layer(t, h) for h in range(2)]
        while turns:
            turns = [g for g in turns if next(g, "done") is None]
        return carry

    lax.fori_loop(0, STEPS, step, 0)

    for i in range(n):
        osend[i] = rows[4 * i : 4 * i + 4, :].astype(BF)

    def o_copy(d):
        p = (e + d) % n
        return remote(
            osend.at[place(p // NZ, p % NZ)], obuf.at[e], o_sem.at[0], o_sem.at[1], {"expert": p}
        )

    def send_out(d, _):
        o_copy(d).start()
        return 0

    lax.fori_loop(1, n, send_out, 0)
    own_o = pltpu.make_async_copy(osend.at[mine], obuf.at[e], o_sem.at[2])
    own_o.start()
    for t in range(STEPS):
        for d in range(1, NY):
            for c in kv_copies(t, d):
                c.wait_send()
    for i in range(2):
        for d in range(1, NY):
            weight_copy(i, d).wait_send()
    many(hbuf, n - 1, sm_send.at[0], sm_recv.at[0]).wait_send()
    many(mbuf, n - 1, sm_send.at[1], sm_recv.at[1]).wait_send()
    own_o.wait()
    many(obuf, n - 1, o_sem.at[0], o_sem.at[1]).wait_recv()
    for i in range(n):
        out[:, 128 * i : 128 * i + 128] = obuf[i]
    many(obuf, n - 1, o_sem.at[0], o_sem.at[1]).wait_send()


def body(
    hidden_in, attn_gain, w_query, w_out, key_cache, value_cache, lengths, ffn_gain,
    w_gate, w_up, w_down, routes, gates,
):
    def by_head(cache):
        return cache[0].transpose(3, 0, 1, 2, 4).reshape(NY, STEPS, 256, 128)

    DMA = pltpu.SemaphoreType.DMA
    V = pltpu.VMEM
    scratch = [
        V((1024, 512), BF), V((1024, 512), BF), V((4096, 768), BF), V((384, 4096), BF),
        V((1, 4096), BF), V((1, 4096), BF),
        V((STEPS, NY, 256, 128), BF), V((STEPS, NY, 256, 128), BF),
        V((STEPS, 4, 8), jnp.int32), V((STEPS, 4, 8), F32), V((STEPS, 4), jnp.int32), V((4, 128), F32),
        V((32, 4, 128), BF), V((32, 4, 128), F32), V((128, 128), F32), V((128, 128), F32),
        V((STEPS, 2, NZ, 64, 128), BF),
        V((STEPS, 2, NZ, 8, 8, 128), BF), V((STEPS, 2, NY, NZ, 64, 128), BF),
        V((STEPS, 2, 32, 8, 128), BF), V((STEPS, 2, 32, 8, 128), BF),
        V((STEPS, 2, 8, 128), F32), V((STEPS, 2, NY, 8, 128), F32),
        V((STEPS, 2, NY, 64, 128), BF), V((STEPS, 2, 3, 64, 128), BF),
        V((STEPS, 2, NY, NZ, 64, 128), BF), V((STEPS, 2, 3, NZ, 64, 128), BF),
        V((STEPS, 2, NZ, 64, 128), BF), V((STEPS, 2, NZ, 64, 128), BF),
        V((2, 64, 128), F32), V((2, 64, 896), F32), V((2, 64, 384), BF),
        V((32, 4, 128), BF), V((32, 4, 128), BF),
        DMA((10,)), DMA((2, NY)), DMA((2, NY)),
        DMA((2, STEPS)), DMA((2, STEPS, NY)), DMA((2, STEPS, NY)),
        DMA((2,)), DMA((2,)), DMA((2,)),
        DMA((3, 2, NZ)), DMA((3, STEPS, 2, NZ)),
        DMA((2, 3, 3)), DMA((STEPS, 2, 3, 3)),
        DMA((2, 2)), DMA((2,)), DMA((STEPS, 2)),
        DMA((2, NY)), DMA((STEPS, 2, NY)), DMA((2, 3)), DMA((STEPS, 2, 3)),
        DMA((2, 2, 3)), DMA((STEPS, 2, 2, 3)),
        DMA((2, NZ)), DMA((STEPS, 2, NZ)),
        DMA((3,)),
    ]
    hbm = pl.BlockSpec(memory_space=pl.ANY)
    out = pl.pallas_call(
        kernel,
        out_shape=jax.ShapeDtypeStruct((4, 4096), BF),
        in_specs=[hbm] * 13,
        out_specs=pl.BlockSpec(memory_space=pltpu.VMEM),
        scratch_shapes=scratch,
        compiler_params=pltpu.CompilerParams(
            collective_id=0, has_side_effects=True, vmem_limit_bytes=60 * 1024 * 1024
        ),
        name="relay_layers",
    )(
        hidden_in[0], routes[0], gates[0], lengths[0], attn_gain, ffn_gain, w_query[0], w_out[0], w_gate[0, 0], w_up[0, 0], w_down[0, 0],
        by_head(key_cache), by_head(value_cache),
    )
    return out[None]


def solution(mesh):
    return jax.shard_map(
        body,
        mesh=mesh,
        in_specs=(
            P("section", "expert", None),
            P("section", None),
            P("section", None, "expert"),
            P("section", None, "expert"),
            P("section", None, "expert", None, None, None),
            P("section", None, "expert", None, None, None),
            P("section", None, "expert"),
            P("section", None),
            P("section", "expert", None, None),
            P("section", "expert", None, None),
            P("section", "expert", None, None),
            P("section", None, "expert", None),
            P("section", None, "expert", None),
        ),
        out_specs=P("section", "expert", None),
        check_vma=False,
    )
```

```python
import jax
import jax.numpy as jnp
from jax import lax
from jax.experimental import pallas as pl
from jax.experimental.pallas import tpu as pltpu
from jax.sharding import PartitionSpec as P

STEPS = 3
NY = 4
NZ = 8
EPS = 1e-06
NEAR_FIRST = (0, 1, 7, 2, 6, 3, 5, 4)
FAR_FIRST = (4, 3, 5, 2, 6, 1, 7, 0)
BF = jnp.bfloat16
F32 = jnp.float32
MESH = pl.DeviceIdType.MESH


def remote(src, dst, send, recv, peer):
    return pltpu.make_async_remote_copy(
        src_ref=src, dst_ref=dst, send_sem=send, recv_sem=recv, device_id=peer, device_id_type=MESH
    )


def pieces_to_rows(pieces, rows):
    for i in range(pieces.shape[0]):
        rows[4 * i : 4 * i + 4, :] = pieces[i].astype(F32)


def kernel(
    hid, routes, gates, lens, again, fgain, wq, wo, wg, wu, wd, kt, vt,
    out,
    wq_v, wo_v, wgu_v, wd_v, ga_v, gf_v, kraw, vraw, ksort, vsort, kbuf, vbuf,
    r_v, g_v, l_v, meta, hbuf, mbuf, rows, mrows, xg, ctx, grid, qsend, qbuf, ssend, sbuf, opart, o_in, part, y_in, ysum, zin,
    mid, acc, act, osend, obuf,
    load_sem, w_send, w_recv, kv_own, kv_send, kv_recv, sm_own, sm_send, sm_recv,
    z_send, z_recv, y_send, y_recv,
    q_own, q_snd, q_rcv, s_snd, s_rcv, ao_send, ao_recv, ry_send, ry_recv, rz_send, rz_recv,
    o_sem,
):
    e = lax.axis_index("expert")
    s = lax.axis_index("section")
    y, z = e // NZ, e % NZ
    nsec = lax.axis_size("section")
    n = NY * NZ
    nxt, prv = (s + 1) % nsec, (s + nsec - 1) % nsec
    up, down, far = (y + 1) % NY, (y + NY - 1) % NY, (y + 2) % NY
    d_model = n * 128
    H = 64

    def dev(yy, zz):
        return {"expert": yy * NZ + zz}

    def place(yy, zz):
        return (yy // 2) * 16 + zz * 2 + yy % 2

    loads = [
        pltpu.make_async_copy(again, ga_v, load_sem.at[0]),
        pltpu.make_async_copy(fgain, gf_v, load_sem.at[1]),
        pltpu.make_async_copy(wg, wgu_v.at[:, 0:384], load_sem.at[2]),
        pltpu.make_async_copy(wu, wgu_v.at[:, 384:768], load_sem.at[3]),
        pltpu.make_async_copy(wd, wd_v, load_sem.at[4]),
        pltpu.make_async_copy(routes, r_v, load_sem.at[7]),
        pltpu.make_async_copy(gates, g_v, load_sem.at[8]),
        pltpu.make_async_copy(lens, l_v, load_sem.at[9]),
        pltpu.make_async_copy(kt, kraw, load_sem.at[10]),
        pltpu.make_async_copy(vt, vraw, load_sem.at[11]),
    ]

    def quarter(w, w_v, yy):
        return (
            w.at[pl.ds(pl.multiple_of(1024 * yy, 1024), 1024), :],
            w_v.at[:, pl.ds(pl.multiple_of(128 * y, 128), 128)],
        )

    def own_weight(i):
        return pltpu.make_async_copy(*quarter((wq, wo)[i], (wq_v, wo_v)[i], y), load_sem.at[5 + i])

    def weight_copy(i, d):
        yy = (y + d) % NY
        return remote(
            *quarter((wq, wo)[i], (wq_v, wo_v)[i], yy), w_send.at[i, d], w_recv.at[i, d], dev(yy, z)
        )

    for c in loads[5:10]:
        c.start()
    own_weight(0).start()
    own_weight(1).start()
    for c in loads[0:5]:
        c.start()

    barrier = pltpu.get_barrier_semaphore()

    def greet(d, _):
        pl.semaphore_signal(barrier, inc=1, device_id={"expert": (e + d) % n}, device_id_type=MESH)
        return 0

    lax.fori_loop(1, n, greet, 0)

    def greet_section(zz, _):
        for sec in (nxt, prv):
            pl.semaphore_signal(
                barrier, inc=1, device_id={"section": sec, "expert": y * NZ + zz}, device_id_type=MESH
            )
        return 0

    lax.fori_loop(0, NZ, greet_section, 0)

    for c in loads[5:8]:
        c.wait()
    slot = lax.broadcasted_iota(jnp.int32, (4, 128), 1)
    eye = lax.broadcasted_iota(jnp.int32, (4, 4), 0) == lax.broadcasted_iota(jnp.int32, (4, 4), 1)
    table = jnp.zeros((4, 128), F32)
    for t in range(STEPS):
        share = g_v[t] / jnp.sum(g_v[t], axis=1, keepdims=True)
        for k in range(8):
            table = table + jnp.where(slot == r_v[t][:, k : k + 1] + 16 * t, share[:, k : k + 1], 0.0)
        length = jnp.sum(jnp.where(eye, l_v[t : t + 1, :].astype(F32), 0.0), axis=1, keepdims=True)
        table = table + jnp.where(slot == 64 + t, length, 0.0)
    meta[...] = table
    pl.semaphore_wait(barrier, n - 1 + 2 * NZ)

    mine = place(y, z)

    def hid_copy(p):
        return remote(
            hid.at[:, pl.ds(pl.multiple_of(128 * p, 128), 128)], hbuf.at[mine],
            sm_send.at[0], sm_recv.at[0], {"expert": p},
        )

    def meta_copy(p):
        return remote(meta, mbuf.at[mine], sm_send.at[1], sm_recv.at[1], {"expert": p})

    def send_start(d, _):
        hid_copy((e + d) % n).start()
        return 0

    def send_meta(d, _):
        meta_copy((e + d) % n).start()
        return 0

    own_h = pltpu.make_async_copy(
        hid.at[:, pl.ds(pl.multiple_of(128 * e, 128), 128)], hbuf.at[mine], sm_own.at[0]
    )
    own_m = pltpu.make_async_copy(meta, mbuf.at[mine], sm_own.at[1])
    own_h.start()
    own_m.start()
    lax.fori_loop(1, n, send_start, 0)

    def kv_copies(t, d):
        yy = (y + d) % NY
        return (
            remote(ksort.at[yy, t], kbuf.at[t, y], kv_send.at[0, t, d], kv_recv.at[0, t, d], dev(yy, z)),
            remote(vsort.at[yy, t], vbuf.at[t, y], kv_send.at[1, t, d], kv_recv.at[1, t, d], dev(yy, z)),
        )

    def kv_owns(t):
        return (
            pltpu.make_async_copy(ksort.at[y, t], kbuf.at[t, y], kv_own.at[0, t]),
            pltpu.make_async_copy(vsort.at[y, t], vbuf.at[t, y], kv_own.at[1, t]),
        )

    def send_caches(t):
        i = lax.broadcasted_iota(jnp.int32, (256, 256), 0)
        j = lax.broadcasted_iota(jnp.int32, (256, 256), 1)
        order = jnp.where(jnp.logical_and(j % 4 == i // 64, j // 4 == i % 64), 1.0, 0.0).astype(BF)
        for raw, sort in ((kraw, ksort), (vraw, vsort)):
            for r in range(4):
                res = jnp.dot(order, raw[t, 256 * r : 256 * r + 256, :], preferred_element_type=F32).astype(BF)
                for yy in range(NY):
                    sort[yy, t, 64 * r : 64 * r + 64, :] = res[64 * yy : 64 * yy + 64, :]
        for c in kv_owns(t):
            c.start()
        for d in range(1, NY):
            for c in kv_copies(t, d):
                c.start()

    for d in range(1, NY):
        weight_copy(0, d).start()
    for c in loads[8:10]:
        c.wait()
    send_caches(0)
    lax.fori_loop(1, n, send_meta, 0)

    def many(ref, k, send, recv):
        view = ref.at[pl.ds(0, k)]
        return remote(view, view, send, recv, {"expert": (e + 1) % n})

    own_h.wait()
    many(hbuf, n - 1, sm_send.at[0], sm_recv.at[0]).wait_recv()
    pieces_to_rows(hbuf, rows)
    for h in range(2):
        xg[0, h, z] = rows[H * h : H * h + H, :].astype(BF)

    def from_z(d):
        return (z + NZ - d) % NZ

    class RowGather:
        def __init__(self, g, t, h, buf):
            self.g, self.t, self.h, self.buf = g, t, h, buf

        def z_copy(self, d):
            b = self.buf.at[self.t, self.h, z]
            return remote(
                b, b, z_send.at[self.g, self.h, d], z_recv.at[self.g, self.t, self.h, d], dev(y, to(d))
            )

        def issue(self):
            for d in NEAR_FIRST[1:]:
                self.z_copy(d).start()

        def take(self):
            for d in NEAR_FIRST[1:]:
                self.z_copy(d).wait_recv()

        def drain(self):
            for d in NEAR_FIRST[1:]:
                self.z_copy(d).wait_send()

    class Gather:
        GROUPS = ((0, 1), (1, 5), (5, 8))

        def __init__(self, t, h):
            self.t, self.h = t, h

        def z_copy(self, k):
            return remote(
                grid.at[self.t, self.h, y, 0], grid.at[self.t, self.h, y, k],
                z_send.at[2, self.h, k], z_recv.at[2, self.t, self.h, k], dev(y, to(NEAR_FIRST[k])),
            )

        def y_copy(self, i, way):
            first, last = self.GROUPS[i]
            b = grid.at[self.t, self.h, y, pl.ds(first, last - first)]
            return remote(
                b, b, y_send.at[self.h, i, way], y_recv.at[self.t, self.h, i, way], dev((far, up, down)[way], z)
            )

        def forward_group(self, i):
            for way in range(3):
                self.y_copy(i, way).start()

        def issue(self):
            for k in range(1, NZ):
                self.z_copy(k).start()
            self.forward_group(0)

        def forward(self):
            for i in range(1, 3):
                for k in range(*self.GROUPS[i]):
                    self.z_copy(k).wait_recv()
                self.forward_group(i)

        def take(self, consume):
            for i in range(3):
                for way in range(3):
                    self.y_copy(i, way).wait_recv()
                for k in range(*self.GROUPS[i]):
                    consume(k)

        def drain(self):
            for k in range(1, NZ):
                self.z_copy(k).wait_send()
            for i in range(3):
                for way in range(3):
                    self.y_copy(i, way).wait_send()

    def column_start(zs, yy):
        return pl.multiple_of(128 * (yy * NZ + zs), 128)

    def scaled(xs, gains):
        xs = [x.astype(F32) for x in xs]
        total = sum(jnp.sum(x * x, axis=1, keepdims=True) for x in xs)
        return total, jnp.concatenate([(x * g.astype(F32)).astype(BF) for x, g in zip(xs, gains)], axis=1)

    def weight_rows(w, zs):
        return jnp.concatenate([w[pl.ds(column_start(zs, yy), 128), :] for yy in range(NY)], axis=0)

    def lane_of(values, index):
        lane = lax.broadcasted_iota(jnp.int32, values.shape, 1)
        return jnp.sum(jnp.where(lane == index, values, 0.0), axis=1, keepdims=True)

    def to(d):
        return (z + d) % NZ

    def q_copy(t, h, d):
        p = (e + d) % n
        return remote(qsend.at[t, h, p], qbuf.at[t, h, e], q_snd.at[h], q_rcv.at[t, h], {"expert": p})

    def s_copy(t, h, d):
        yy = (y + d) % NY
        return remote(ssend.at[t, h], sbuf.at[t, h, y], s_snd.at[h, d], s_rcv.at[t, h, d], dev(yy, z))

    def ao_copy(t, h, way):
        peer = (up, down, far)[way]
        return remote(
            opart.at[t, h, peer], o_in.at[t, h, way], ao_send.at[h, way], ao_recv.at[t, h, way], dev(peer, z)
        )

    def ry_copy(t, h, i, way):
        peer = (far, up, down)[way]
        ks = pl.ds(4 * i, 4)
        return remote(
            part.at[t, h, peer, ks], y_in.at[t, h, way, ks],
            ry_send.at[h, i, way], ry_recv.at[t, h, i, way], dev(peer, z),
        )

    def rz_copy(t, h, k, sec):
        return remote(
            ysum.at[t, h, k], zin.at[t, h, k], rz_send.at[h, k], rz_recv.at[t, h, k],
            {"section": sec, "expert": y * NZ + to(FAR_FIRST[k])},
        )

    def layer(t, h):
        ga, gc, gd = RowGather(0, t, h, xg), RowGather(1, t, h, ctx), Gather(t, h)

        @pl.when(t > 0)
        def _():
            state = jnp.zeros((H, 128), F32)
            for k in range(NZ):
                rz_copy(t - 1, h, k, nxt).wait_recv()
                state = state + zin[t - 1, h, k].astype(F32)
            xg[t, h, z] = state.astype(BF)

        ga.issue()
        yield

        ga.take()
        if h == 0:
            @pl.when(t == 0)
            def _():
                loads[0].wait()
                own_weight(0).wait()
                for d in range(1, NY):
                    weight_copy(0, d).wait_recv()

        total, lhs = scaled(
            [xg[t, h, zz] for zz in range(NZ)],
            [ga_v[:, pl.ds(column_start(zz, y), 128)] for zz in range(NZ)],
        )
        query = jnp.dot(lhs, wq_v[...], preferred_element_type=F32)
        for yy in range(NY):
            qsend[t, h, NZ * yy : NZ * yy + NZ] = query[:, 128 * yy : 128 * yy + 128].reshape(NZ, 8, 128).astype(BF)
        acc[h, :, 0:128] = jnp.broadcast_to(total, (H, 128))
        ssend[t, h] = acc[h, pl.ds(pl.multiple_of(8 * z, 8), 8), 0:128]
        own_q = pltpu.make_async_copy(qsend.at[t, h, e], qbuf.at[t, h, e], q_own.at[h, 0])
        own_s = pltpu.make_async_copy(ssend.at[t, h], sbuf.at[t, h, y], q_own.at[h, 1])
        own_q.start()
        own_s.start()

        def send_q(d, _):
            q_copy(t, h, d).start()
            return 0

        lax.fori_loop(1, n, send_q, 0)
        for d in range(1, NY):
            s_copy(t, h, d).start()

        if h == 1:
            @pl.when(t == 0)
            def _():
                for d in range(1, NY):
                    weight_copy(1, d).start()
        yield

        if h == 0:
            for c in kv_owns(t):
                c.wait()
            for d in range(1, NY):
                for c in kv_copies(t, d):
                    c.wait_recv()

            @pl.when(t == 0)
            def _():
                own_m.wait()
                many(mbuf, n - 1, sm_send.at[1], sm_recv.at[1]).wait_recv()
                pieces_to_rows(mbuf, mrows)

        length = lane_of(mrows[pl.ds(pl.multiple_of(H * h + 8 * z, 8), 8), :], 64 + t)
        length = jnp.concatenate([length] * NZ, axis=0)
        key_lane = lax.broadcasted_iota(jnp.int32, (H, 512), 1)
        key_row = lax.broadcasted_iota(jnp.int32, (H, 512), 0)
        own_q.wait()
        own_s.wait()
        many(qbuf.at[t, h], n - 1, q_snd.at[h], q_rcv.at[t, h]).wait_recv()
        for d in range(1, NY):
            s_copy(t, h, d).wait_recv()
        query = sum(qbuf[t, h, NZ * yy : NZ * yy + NZ].astype(F32) for yy in range(NY))
        mean_x = sum(sbuf[t, h, yy] for yy in range(NY)) / d_model
        mean_q = jnp.mean(query * query, axis=2, keepdims=True)
        query = query * lax.rsqrt(mean_q + EPS * (mean_x[None] + EPS))
        qs = query.reshape(H, 128).astype(BF)
        scores = lax.dot_general(
            qs, kbuf[t, 2 * h : 2 * h + 2].reshape(512, 128), (((1,), (1,)), ((), ())),
            preferred_element_type=F32,
        ) * (128 ** -0.5)
        valid = jnp.logical_and(key_lane // 64 == key_row % 8, (key_lane % 64).astype(F32) < length)
        exps = jnp.where(valid, jnp.exp(scores), 0.0)
        weights = (exps / jnp.sum(exps, axis=1, keepdims=True)).astype(BF)
        context = jnp.dot(weights, vbuf[t, 2 * h : 2 * h + 2].reshape(512, 128), preferred_element_type=F32)
        ctx[t, h, z] = context.reshape(NZ, 8, 128).astype(BF)
        gc.issue()
        yield

        gc.take()
        if h == 0:
            @pl.when(t == 0)
            def _():
                own_weight(1).wait()
                for d in range(1, NY):
                    weight_copy(1, d).wait_recv()

        lhs = jnp.concatenate(
            [ctx[t, h, :, hh].astype(F32).reshape(H, 128).astype(BF) for hh in range(NZ)], axis=1
        )
        attended = jnp.dot(lhs, wo_v[...], preferred_element_type=F32)
        for yy in range(NY):
            opart[t, h, yy] = attended[:, 128 * yy : 128 * yy + 128].astype(BF)
        for way in range(3):
            ao_copy(t, h, way).start()
        yield
        middle = xg[t, h, z].astype(F32) + opart[t, h, y].astype(F32)
        for way in range(3):
            ao_copy(t, h, way).wait_recv()
            middle = middle + o_in[t, h, way].astype(F32)
        mid[h] = middle
        grid[t, h, y, 0] = middle.astype(BF)
        gd.issue()
        yield
        gd.forward()
        yield
        if h == 0:
            @pl.when(t == 0)
            def _():
                for c in loads[1:5]:
                    c.wait()

        acc[h] = jnp.zeros((H, 896), F32)

        def take_ffn(k):
            zs = from_z(NEAR_FIRST[k])
            total, lhs = scaled(
                [grid[t, h, yy, k] for yy in range(NY)],
                [gf_v[:, pl.ds(column_start(zs, yy), 128)] for yy in range(NY)],
            )
            acc[h, :, 0:768] += jnp.dot(lhs, weight_rows(wgu_v, zs), preferred_element_type=F32)
            acc[h, :, 768:896] += jnp.broadcast_to(total, (H, 128))

        gd.take(take_ffn)
        scale = lax.rsqrt(acc[h, :, 768:769] / d_model + EPS)
        share = lane_of(mrows[H * h : H * h + H, :], t * 16 + e // 2)
        gate = acc[h, :, 0:384] * scale
        upv = acc[h, :, 384:768] * scale
        act[h] = (gate / (1.0 + jnp.exp(-gate)) * upv * share).astype(BF)

        for i in range(2):
            for k in range(4 * i, 4 * i + 4):
                zs = to(FAR_FIRST[k])
                w = jnp.concatenate([wd_v[:, pl.ds(column_start(zs, yy), 128)] for yy in range(NY)], axis=1)
                res = jnp.dot(act[h], w, preferred_element_type=F32).astype(BF)
                for yy in range(NY):
                    part[t, h, yy, k] = res[:, 128 * yy : 128 * yy + 128]
            for way in range(3):
                ry_copy(t, h, i, way).start()
        yield
        for i in range(2):
            for way in range(3):
                ry_copy(t, h, i, way).wait_recv()
            for k in range(4 * i, 4 * i + 4):
                total = part[t, h, y, k].astype(F32)
                for way in range(3):
                    total = total + y_in[t, h, way, k].astype(F32)
                if k == NZ - 1:
                    total = total + mid[h]
                    mid[h] = total
                ysum[t, h, k] = total.astype(BF)

                @pl.when(t < STEPS - 1)
                def _():
                    rz_copy(t, h, k, nxt).start()

                if k < NZ - 1:
                    @pl.when(t == STEPS - 1)
                    def _():
                        rz_copy(t, h, k, s).start()
        if h == 1:
            @pl.when(t < STEPS - 1)
            def _():
                send_caches(t + 1)
        yield

        @pl.when(t == STEPS - 1)
        def _():
            result = mid[h]
            for k in range(NZ - 1):
                rz_copy(t, h, k, s).wait_recv()
                result = result + zin[t, h, k].astype(F32)
            rows[H * h : H * h + H, :] = result

        yield
        ga.drain()
        gc.drain()
        gd.drain()
        many(qbuf.at[t, h], n - 1, q_snd.at[h], q_rcv.at[t, h]).wait_send()
        for d in range(1, NY):
            s_copy(t, h, d).wait_send()
        for way in range(3):
            ao_copy(t, h, way).wait_send()
        for i in range(2):
            for way in range(3):
                ry_copy(t, h, i, way).wait_send()
        for k in range(NZ - 1):
            rz_copy(t, h, k, nxt).wait_send()

        @pl.when(t < STEPS - 1)
        def _():
            rz_copy(t, h, NZ - 1, nxt).wait_send()

    def step(t, carry):
        turns = [layer(t, h) for h in range(2)]
        while turns:
            turns = [g for g in turns if next(g, "done") is None]
        return carry

    lax.fori_loop(0, STEPS, step, 0)

    for i in range(n):
        osend[i] = rows[4 * i : 4 * i + 4, :].astype(BF)

    def o_copy(d):
        p = (e + d) % n
        return remote(
            osend.at[place(p // NZ, p % NZ)], obuf.at[e], o_sem.at[0], o_sem.at[1], {"expert": p}
        )

    def send_out(d, _):
        o_copy(d).start()
        return 0

    lax.fori_loop(1, n, send_out, 0)
    own_o = pltpu.make_async_copy(osend.at[mine], obuf.at[e], o_sem.at[2])
    own_o.start()
    for t in range(STEPS):
        for d in range(1, NY):
            for c in kv_copies(t, d):
                c.wait_send()
    for i in range(2):
        for d in range(1, NY):
            weight_copy(i, d).wait_send()
    many(hbuf, n - 1, sm_send.at[0], sm_recv.at[0]).wait_send()
    many(mbuf, n - 1, sm_send.at[1], sm_recv.at[1]).wait_send()
    own_o.wait()
    many(obuf, n - 1, o_sem.at[0], o_sem.at[1]).wait_recv()
    for i in range(n):
        out[:, 128 * i : 128 * i + 128] = obuf[i]
    many(obuf, n - 1, o_sem.at[0], o_sem.at[1]).wait_send()


def body(
    hidden_in, attn_gain, w_query, w_out, key_cache, value_cache, lengths, ffn_gain,
    w_gate, w_up, w_down, routes, gates,
):
    DMA = pltpu.SemaphoreType.DMA
    V = pltpu.VMEM
    scratch = [
        V((1024, 512), BF), V((1024, 512), BF), V((4096, 768), BF), V((384, 4096), BF),
        V((1, 4096), BF), V((1, 4096), BF),
        V((STEPS, 1024, 128), BF), V((STEPS, 1024, 128), BF),
        V((NY, STEPS, 256, 128), BF), V((NY, STEPS, 256, 128), BF),
        V((STEPS, NY, 256, 128), BF), V((STEPS, NY, 256, 128), BF),
        V((STEPS, 4, 8), jnp.int32), V((STEPS, 4, 8), F32), V((STEPS, 4), jnp.int32), V((4, 128), F32),
        V((32, 4, 128), BF), V((32, 4, 128), F32), V((128, 128), F32), V((128, 128), F32),
        V((STEPS, 2, NZ, 64, 128), BF),
        V((STEPS, 2, NZ, 8, 8, 128), BF), V((STEPS, 2, NY, NZ, 64, 128), BF),
        V((STEPS, 2, 32, 8, 128), BF), V((STEPS, 2, 32, 8, 128), BF),
        V((STEPS, 2, 8, 128), F32), V((STEPS, 2, NY, 8, 128), F32),
        V((STEPS, 2, NY, 64, 128), BF), V((STEPS, 2, 3, 64, 128), BF),
        V((STEPS, 2, NY, NZ, 64, 128), BF), V((STEPS, 2, 3, NZ, 64, 128), BF),
        V((STEPS, 2, NZ, 64, 128), BF), V((STEPS, 2, NZ, 64, 128), BF),
        V((2, 64, 128), F32), V((2, 64, 896), F32), V((2, 64, 384), BF),
        V((32, 4, 128), BF), V((32, 4, 128), BF),
        DMA((12,)), DMA((2, NY)), DMA((2, NY)),
        DMA((2, STEPS)), DMA((2, STEPS, NY)), DMA((2, STEPS, NY)),
        DMA((2,)), DMA((2,)), DMA((2,)),
        DMA((3, 2, NZ)), DMA((3, STEPS, 2, NZ)),
        DMA((2, 3, 3)), DMA((STEPS, 2, 3, 3)),
        DMA((2, 2)), DMA((2,)), DMA((STEPS, 2)),
        DMA((2, NY)), DMA((STEPS, 2, NY)), DMA((2, 3)), DMA((STEPS, 2, 3)),
        DMA((2, 2, 3)), DMA((STEPS, 2, 2, 3)),
        DMA((2, NZ)), DMA((STEPS, 2, NZ)),
        DMA((3,)),
    ]
    hbm = pl.BlockSpec(memory_space=pl.ANY)
    out = pl.pallas_call(
        kernel,
        out_shape=jax.ShapeDtypeStruct((4, 4096), BF),
        in_specs=[hbm] * 13,
        out_specs=pl.BlockSpec(memory_space=pltpu.VMEM),
        scratch_shapes=scratch,
        compiler_params=pltpu.CompilerParams(
            collective_id=0, has_side_effects=True, vmem_limit_bytes=60 * 1024 * 1024
        ),
        name="relay_layers",
    )(
        hidden_in[0], routes[0], gates[0], lengths[0], attn_gain, ffn_gain, w_query[0], w_out[0], w_gate[0, 0], w_up[0, 0], w_down[0, 0],
        key_cache[0].reshape(STEPS, 1024, 128), value_cache[0].reshape(STEPS, 1024, 128),
    )
    return out[None]


def solution(mesh):
    return jax.shard_map(
        body,
        mesh=mesh,
        in_specs=(
            P("section", "expert", None),
            P("section", None),
            P("section", None, "expert"),
            P("section", None, "expert"),
            P("section", None, "expert", None, None, None),
            P("section", None, "expert", None, None, None),
            P("section", None, "expert"),
            P("section", None),
            P("section", "expert", None, None),
            P("section", "expert", None, None),
            P("section", "expert", None, None),
            P("section", None, "expert", None),
            P("section", None, "expert", None),
        ),
        out_specs=P("section", "expert", None),
        check_vma=False,
    )
```
